256 devices in a mesh: ty: 8 (over y, x_lo), tx: 32 (over z, x_hi, core).
Axes of the slice: x: 4 (x_hi: 2, x_lo: 2; x = x_hi * 2 + x_lo), y: 4, z: 8, core: 2. Of those that a mesh axis runs over, the one named last changes fastest.
Arguments:
- sky: bfloat16 [4096, 16384], P('ty', 'tx'), may hold values from -6 to 6
- point_count: int32 [8, 32], P('ty', 'tx'), may hold values from 0 to 4, as said below
- point_offset: int32 [8, 32, 4, 2], P('ty', 'tx'), may hold values from 0 to 511
- beam_width: bfloat16 [8, 32, 4], P('ty', 'tx'), may hold values from 128 to 340
- uv_bins: int32 [8, 32, 4, 2, 2], P('ty', 'tx'), may hold values from 0 to 7
- uv_count: int32 [8, 32, 4], P('ty', 'tx'), may hold values from 1 to 2
- uv_weight: bfloat16 [8, 32, 4, 2, 128, 128], P('ty', 'tx'), may hold values from 1 to 8
Outputs:
- curvature: float32 [4096, 16384], P('ty', 'tx')
The draws below stay inside these ranges and needn't reach their ends.
Inputs may be any that keep to these rules, and one draw needn't show every extreme that they name: `point_count`: each tile holds at most 4 pointings, and the tiles of columns 2i and 2i + 1 of one row hold at most 4 together; in every draw some such pair holds exactly 4, all on one of its tiles. `point_offset`: entries of slots at or beyond a tile's count are ignored. `uv_bins`: entries of uv slots at or beyond a pointing's uv_count are ignored.
All inputs are finite; a program needn't handle non-finite values.
Results may differ from the reference program's by a relative error of at most 0.0085.
Values may be sent and summed in bfloat16 or wider, within the bound.
No kernel may reach another device: no remote copies, remote signals or barrier semaphores. Data moves between devices by JAX's collectives and lax.ppermute only.
A program may use at most 128 MiB of HBM per device.

```python
import math
import jax
import jax.numpy as jnp
from jax import lax

TILE = 512
UVB = 128
UVSLOT = 2
SLOTS = 4
UVBLK = 8
GRID_Y = 8
GRID_X = 32
SKY_Y = 4096
SKY_X = 16384


def draw_point_count(key, part):
    key_total, key_first, key_where, key_side = jax.random.split(jax.random.fold_in(key, 11), 4)
    pairs = GRID_X // 2
    totals = jax.random.randint(key_total, (GRID_Y, pairs), 2, SLOTS + 1)
    first = jax.random.randint(key_first, (GRID_Y, pairs), 0, totals + 1)
    chosen = jax.random.randint(key_where, (), 0, GRID_Y * pairs)
    side = jax.random.randint(key_side, (), 0, 2)
    flat = jnp.arange(GRID_Y * pairs, dtype=jnp.int32).reshape(GRID_Y, pairs)
    hit = flat == chosen
    totals = jnp.where(hit, SLOTS, totals)
    first = jnp.where(hit, side * SLOTS, first)
    second = totals - first
    return jnp.stack([first, second], axis=-1).reshape(GRID_Y, GRID_X).astype(jnp.int32)


def set_ends(entries, stream_key, smallest, high):
    extent = entries.shape
    spot = [jax.random.randint(jax.random.fold_in(stream_key, axis), (), 0, extent[axis]) for axis in range(len(extent))]
    entries = entries.at[tuple(spot)].set(smallest)
    longest = extent.index(max(extent))
    spot[longest] = (spot[longest] + 1) % extent[longest]
    return entries.at[tuple(spot)].set(high)


def level_of(rng, shape, shards, low, largest):
    level, own = 1.0, jax.random.fold_in(rng, 6)
    for dim, shards_of in shards:
        heights = jnp.exp(jax.random.uniform(jax.random.fold_in(own, dim), (shards_of,), jnp.float32, low / len(shards), largest / len(shards)))
        level = level * jnp.repeat(heights, shape[dim] // shards_of).reshape([-1 if axis == dim else 1 for axis in range(len(shape))])
    return level


def normal_values(rng, extent, scale, limit, cuts=(), kind=jnp.bfloat16):
    values = jax.random.normal(rng, extent, jnp.float32) * scale
    if len(cuts) > 0:
        values = level_of(rng, extent, cuts, -0.22, 0.18) * values
    return jnp.clip(values, min=-limit, max=limit).astype(kind)


def setup_inputs(seed: int = 0) -> dict:
    keys = jax.random.split(jax.random.key(seed), 8)
    sky = normal_values(keys[0], (SKY_Y, SKY_X), 1.0, 6.0, ((0, 8), (1, 32)))
    point_count = draw_point_count(jax.random.fold_in(keys[7], 71), 0)
    point_offset = set_ends(jax.random.randint(keys[2], (GRID_Y, GRID_X, SLOTS, 2), 0, TILE), jax.random.fold_in(keys[2], 1), 0, TILE - 1).astype(jnp.int32)
    beam_width = jnp.clip(jnp.exp(math.log(340.0) - 0.97691535 * jax.random.uniform(keys[3], (GRID_Y, GRID_X, SLOTS), jnp.float32) ** level_of(keys[3], (GRID_Y, GRID_X, SLOTS), ((0, 8), (1, 32)), -0.2, 0.2)), 128.0, 340.0).astype(jnp.bfloat16)
    uv_bins = set_ends(jax.random.randint(keys[4], (GRID_Y, GRID_X, SLOTS, UVSLOT, 2), 0, UVBLK), jax.random.fold_in(keys[4], 1), 0, UVBLK - 1).astype(jnp.int32)
    uv_count = set_ends(jax.random.randint(keys[5], (GRID_Y, GRID_X, SLOTS), 1, UVSLOT + 1), jax.random.fold_in(keys[5], 1), 1, UVSLOT).astype(jnp.int32)
    uv_weight = jnp.clip(jnp.exp(math.log(8.0) - 2.0794415 * jax.random.uniform(keys[6], (GRID_Y, GRID_X, SLOTS, UVSLOT, UVB, UVB), jnp.float32) ** level_of(keys[6], (GRID_Y, GRID_X, SLOTS, UVSLOT, UVB, UVB), ((0, 8), (1, 32)), -0.2, 0.2)), 1.0, 8.0).astype(jnp.bfloat16)
    return {"sky": sky, "point_count": point_count, "point_offset": point_offset, "beam_width": beam_width, "uv_bins": uv_bins, "uv_count": uv_count, "uv_weight": uv_weight}


def dft_tables(blocks, block_size, length):
    rows = blocks[:, None] * block_size + jnp.arange(block_size, dtype=jnp.int32)[None, :]
    pixels = jnp.arange(length, dtype=jnp.int32)
    phase = rows[:, :, None] * pixels[None, None, :] % length
    angle = phase.astype(jnp.float32) * (2.0 * math.pi / length)
    factor = 1.0 / math.sqrt(length)
    return ((jnp.cos(angle) * factor).astype(jnp.bfloat16), (jnp.sin(angle) * factor).astype(jnp.bfloat16))

def beam_map(width, length):
    offset = jnp.arange(length, dtype=jnp.float32) - length // 2
    square = offset * offset
    radius = square[:, None] + square[None, :]
    spread = width.astype(jnp.float32)
    return jnp.exp(-radius / (2.0 * spread * spread))

def pointing_image(beamed, width, uv_pair, used, weight_tiles):
    slots_uv = weight_tiles.shape[0]
    block_size = weight_tiles.shape[1]
    length = beamed.shape[0]
    row_cos, row_sin = dft_tables(uv_pair[:, 0], block_size, length)
    col_cos, col_sin = dft_tables(uv_pair[:, 1], block_size, length)
    row_tables = jnp.stack([row_cos, row_sin], axis=1).reshape(slots_uv * 2 * block_size, length)
    col_tables = jnp.stack([jnp.concatenate([col_cos, col_sin], axis=1), jnp.concatenate([-col_sin, col_cos], axis=1)], axis=1)
    first = jnp.dot(row_tables, beamed, preferred_element_type=jnp.float32).astype(jnp.bfloat16)
    first = first.reshape(slots_uv, 2, block_size, length)
    visible = jnp.einsum('kcin,kcbn->kib', first.astype(jnp.float32), col_tables.astype(jnp.float32))
    used_mask = (jnp.arange(slots_uv, dtype=jnp.int32) < used).astype(jnp.float32)
    weighted = weight_tiles.astype(jnp.float32) * used_mask[:, None, None]
    scaled = (visible * jnp.concatenate([weighted, weighted], axis=2)).astype(jnp.bfloat16)
    spread = jnp.einsum('kib,kcbn->kcin', scaled.astype(jnp.float32), col_tables.astype(jnp.float32))
    spread = spread.astype(jnp.bfloat16).reshape(slots_uv * 2 * block_size, length)
    back = lax.dot_general(row_tables, spread, (((0,), (0,)), ((), ())), preferred_element_type=jnp.float32)
    return (beam_map(width, length) * back).astype(jnp.bfloat16)

def reference(sky, point_count, point_offset, beam_width, uv_bins, uv_count, uv_weight):
    grid_rows, grid_cols = point_count.shape
    slots = point_offset.shape[2]
    tile_size = TILE
    patch_size = 2 * TILE
    padded = jnp.pad(sky, tile_size)
    pairs = grid_cols // 2
    shape = (grid_rows, pairs, slots)
    row_ids = jnp.broadcast_to(jnp.arange(grid_rows, dtype=jnp.int32)[:, None, None], shape)
    pair_ids = jnp.broadcast_to(jnp.arange(pairs, dtype=jnp.int32)[None, :, None], shape)
    combined = jnp.broadcast_to(jnp.arange(slots, dtype=jnp.int32)[None, None, :], shape)
    even_count = point_count[:, 0::2][:, :, None]
    odd_count = point_count[:, 1::2][:, :, None]
    from_odd = (combined >= even_count).astype(jnp.int32)
    columns = 2 * pair_ids + from_odd
    slot_ids = jnp.clip(combined - from_odd * even_count, 0, slots - 1)
    live_ids = combined < even_count + odd_count

    def place(total, item):
        row, col, slot, live = item
        offset = point_offset[row, col, slot]
        top = (row * tile_size + offset[0]).astype(jnp.int32)
        left = (col * tile_size + offset[1]).astype(jnp.int32)
        window = lax.dynamic_slice(padded, (top, left), (patch_size, patch_size))
        width = beam_width[row, col, slot]
        beamed = (beam_map(width, patch_size) * window.astype(jnp.float32)).astype(jnp.bfloat16)
        image = pointing_image(beamed, width, uv_bins[row, col, slot], uv_count[row, col, slot], uv_weight[row, col, slot])
        image = jnp.where(live, image.astype(jnp.float32), jnp.zeros((), jnp.float32))
        current = lax.dynamic_slice(total, (top, left), (patch_size, patch_size))
        return (lax.dynamic_update_slice(total, current + image, (top, left)), None)
    start = jnp.zeros(padded.shape, jnp.float32)
    items = (row_ids.reshape(-1), columns.reshape(-1), slot_ids.reshape(-1), live_ids.reshape(-1))
    total, unused = lax.scan(place, start, items)
    return total[tile_size:-tile_size, tile_size:-tile_size]
```

```python
import math

import jax
import jax.numpy as jnp
import ml_dtypes
import numpy as np
from jax import lax
from jax.experimental import pallas as pl
from jax.experimental.pallas import tpu as pltpu
from jax.sharding import PartitionSpec as P

TILE = 512
PATCH = 1024
UVB = 128
BLOCKS = 8
SLOTS = 4
ROWS = 64
VMEM_LIMIT = 56 * 1024 * 1024

COUNT, OFFSET, WIDTH, BINS, USED, META = 0, 1, 9, 13, 29, 33

f32 = jnp.float32
bf16 = jnp.bfloat16


def tables():
    phase = np.outer(np.arange(PATCH), np.arange(PATCH)) % PATCH
    angle = phase * (2.0 * math.pi / PATCH)
    factor = 1.0 / math.sqrt(PATCH)
    cos = (np.cos(angle) * factor).reshape(BLOCKS, UVB, PATCH)
    sin = (np.sin(angle) * factor).reshape(BLOCKS, UVB, PATCH)
    stacked = np.concatenate([cos, sin], axis=1)
    flipped = stacked.transpose(0, 2, 1)
    return stacked.astype(ml_dtypes.bfloat16), np.ascontiguousarray(flipped).astype(ml_dtypes.bfloat16)


def falloff(square, width):
    return jnp.exp(square * (-0.5 / (width * width)))


def row_factor(start, rows, oy, width):
    s = lax.broadcasted_iota(jnp.int32, (rows, 128), 0) + start
    m = ((s - oy) & (PATCH - 1)).astype(f32) - (PATCH // 2)
    return falloff(m * m, width), s


def col_factor(shift, width):
    n = lax.broadcasted_iota(jnp.int32, (8, TILE), 1) + shift
    inside = (n >= 0) & (n < PATCH)
    d = n.astype(f32) - (PATCH // 2)
    return jnp.where(inside, falloff(d * d, width), 0.0)[:1]


def twiddle(a, b, oy, shift):
    i = lax.broadcasted_iota(jnp.int32, (UVB, UVB), 0) + a * UVB
    j = lax.broadcasted_iota(jnp.int32, (UVB, UVB), 1) + b * UVB
    p = j * shift - i * oy
    quarter = (p + PATCH // 8) >> 8
    x = (p - (quarter << 8)).astype(f32) * (2.0 * math.pi / PATCH)
    y = x * x
    sin = x * (1.0 + y * (-1.0 / 6 + y * (1.0 / 120 - y * (1.0 / 5040))))
    cos = 1.0 + y * (-0.5 + y * (1.0 / 24 + y * (-1.0 / 720 + y * (1.0 / 40320))))
    odd = (quarter & 1) == 1
    c = jnp.where(odd, sin, cos)
    s = jnp.where(odd, cos, sin)
    c = jnp.where(((quarter + 1) & 2) == 2, -c, c)
    s = jnp.where((quarter & 2) == 2, -s, s)
    return c, s


def column_shift(step, ox):
    return TILE * (1 - step) - ox


def tile_steps(ctl):
    side = ctl[1]
    return 1 - 2 * side, 2 * side - 1


def lanes():
    return [slice(lane * 128, lane * 128 + 128) for lane in range(TILE // 128)]


def forward_body(kinds, ctl, metas, sky, stacked_hbm, flipped_hbm, outs, scratch):
    own, pair, far = sky
    stacked, flipped, window, sems = scratch
    copy_s = pltpu.make_async_copy(stacked_hbm, stacked, sems.at[0])
    copy_f = pltpu.make_async_copy(flipped_hbm.at[:, :TILE, :], flipped, sems.at[1])
    copy_s.start()
    copy_f.start()
    copy_s.wait()
    copy_f.wait()
    low = ctl[0]
    near, outer = tile_steps(ctl)
    steps = {"own": 0, "near": near, "outer": outer}
    for kind, meta, out in zip(kinds, metas, outs):

        def pointing(s, carry, step=steps[kind], meta=meta, out=out):
            oy, ox = meta[OFFSET + 2 * s], meta[OFFSET + 2 * s + 1]
            width = meta[WIDTH + s].astype(f32)
            shift = column_shift(step, ox)
            cols = col_factor(shift, width)

            def beam_rows(i, c):
                at = pl.multiple_of(i * ROWS, ROWS)
                here = pl.ds(at, ROWS)
                g, rows = row_factor(at, ROWS, oy, width)
                mine = jnp.where(rows >= oy, 1, 0) != low
                g2, _ = row_factor(at + TILE, ROWS, oy, width)
                there = pl.ds(pl.multiple_of(at + TILE, ROWS), ROWS)
                for part in lanes():
                    h = cols[:, part]
                    x = jnp.where(mine, own[here, part].astype(f32), far[here, part].astype(f32))
                    window[here, part] = (x * g * h).astype(bf16)
                    window[there, part] = (pair[here, part].astype(f32) * g2 * h).astype(bf16)
                return c

            lax.fori_loop(0, TILE // ROWS, beam_rows, 0)

            def uv(k, c):
                a = meta[BINS + 4 * s + 2 * k]
                b = meta[BINS + 4 * s + 2 * k + 1]
                first = jnp.dot(stacked[a], window[...], preferred_element_type=f32).astype(bf16)
                q = jnp.dot(first, flipped[b], preferred_element_type=f32)
                re = q[:UVB, :UVB] - q[UVB:, UVB:]
                im = q[:UVB, UVB:] + q[UVB:, :UVB]
                cos, sin = twiddle(a, b, oy, shift)
                out[s, k, :, :UVB] = (re * cos - im * sin).astype(bf16)
                out[s, k, :, UVB:] = (im * cos + re * sin).astype(bf16)
                return c

            lax.fori_loop(0, meta[USED + s], uv, 0)
            return carry

        lax.fori_loop(0, meta[COUNT], pointing, 0)


def forward(kinds, ctl, metas, sky, stacked, flipped):
    n = len(kinds)

    def kernel(ctl, *refs):
        metas, rest = refs[:n], refs[n:]
        forward_body(kinds, ctl, metas, rest[:3], rest[3], rest[4], rest[5 : 5 + n], rest[5 + n :])

    smem = pl.BlockSpec(memory_space=pltpu.SMEM)
    vmem = pl.BlockSpec(memory_space=pltpu.VMEM)
    hbm = pl.BlockSpec(memory_space=pl.ANY)
    shape = jax.ShapeDtypeStruct((SLOTS, 2, UVB, 2 * UVB), bf16)
    return pl.pallas_call(
        kernel,
        out_shape=[shape] * n,
        in_specs=[smem] * (1 + n) + [vmem] * 3 + [hbm] * 2,
        out_specs=[vmem] * n,
        scratch_shapes=[
            pltpu.VMEM((BLOCKS, 2 * UVB, PATCH), bf16),
            pltpu.VMEM((BLOCKS, TILE, 2 * UVB), bf16),
            pltpu.VMEM((PATCH, TILE), bf16),
            pltpu.SemaphoreType.DMA((2,)),
        ],
        compiler_params=pltpu.CompilerParams(vmem_limit_bytes=VMEM_LIMIT),
        name="forward_" + "_".join(kinds),
    )(ctl, *metas, *sky, stacked, flipped)


def scale(meta, mine, near, outer, weight):
    def kernel(meta, mine, near, outer, weight, out):
        def pointing(s, carry):
            def uv(k, c):
                w = weight[s, k].astype(f32)
                v = mine[s, k].astype(f32) + near[s, k].astype(f32) + outer[s, k].astype(f32)
                out[s, k, :, :UVB] = (v[:, :UVB] * w).astype(bf16)
                out[s, k, :, UVB:] = (v[:, UVB:] * w).astype(bf16)
                return c

            lax.fori_loop(0, meta[USED + s], uv, 0)
            return carry

        lax.fori_loop(0, meta[COUNT], pointing, 0)

    smem = pl.BlockSpec(memory_space=pltpu.SMEM)
    vmem = pl.BlockSpec(memory_space=pltpu.VMEM)
    return pl.pallas_call(
        kernel,
        out_shape=jax.ShapeDtypeStruct((SLOTS, 2, UVB, 2 * UVB), bf16),
        in_specs=[smem] + [vmem] * 4,
        out_specs=vmem,
        compiler_params=pltpu.CompilerParams(vmem_limit_bytes=VMEM_LIMIT),
        name="scale",
    )(meta, mine, near, outer, weight)


def adjoint_tile(low, step, meta, scaled, stacked, flipped, spread, totals):
    own, pair, far = totals

    def pointing(s, carry):
        oy, ox = meta[OFFSET + 2 * s], meta[OFFSET + 2 * s + 1]
        width = meta[WIDTH + s].astype(f32)
        shift = column_shift(step, ox)
        cols = col_factor(shift, width)
        used = meta[USED + s]

        def uv(k, c):
            a = meta[BINS + 4 * s + 2 * k]
            b = meta[BINS + 4 * s + 2 * k + 1]
            cos, sin = twiddle(a, b, oy, shift)
            re = scaled[s, k, :, :UVB].astype(f32)
            im = scaled[s, k, :, UVB:].astype(f32)
            mr = (re * cos + im * sin).astype(bf16)
            mi = (im * cos - re * sin).astype(bf16)
            both = jnp.concatenate(
                [jnp.concatenate([mr, mi], axis=1), jnp.concatenate([mi, -mr], axis=1)], axis=0
            )
            spread[k] = jnp.dot(both, stacked[b], preferred_element_type=f32).astype(bf16)
            return c

        lax.fori_loop(0, used, uv, 0)

        def add(count):
            blocks = [meta[BINS + 4 * s + 2 * k] for k in range(count)]
            big = 256

            def image(at):
                back = jnp.dot(flipped[blocks[0], pl.ds(at, big), :], spread[0], preferred_element_type=f32)
                for k in range(1, count):
                    back += jnp.dot(
                        flipped[blocks[k], pl.ds(at, big), :], spread[k], preferred_element_type=f32
                    )
                g, rows = row_factor(at, big, oy, width)
                return [back[:, part] * g * cols[:, part] for part in lanes()], rows

            def rows(i, c):
                at = pl.multiple_of(i * big, big)
                here = pl.ds(at, big)
                values, rows = image(at)
                mine = jnp.where(rows >= oy, 1, 0) != low
                for part, v in zip(lanes(), values):
                    own[here, part] = own[here, part] + jnp.where(mine, v, 0.0)
                    far[here, part] = far[here, part] + jnp.where(mine, 0.0, v)
                values, _ = image(pl.multiple_of(at + TILE, big))
                for part, v in zip(lanes(), values):
                    pair[here, part] = pair[here, part] + v
                return c

            lax.fori_loop(0, TILE // big, rows, 0)

        @pl.when(used == 1)
        def _():
            add(1)

        @pl.when(used == 2)
        def _():
            add(2)

        return carry

    lax.fori_loop(0, meta[COUNT], pointing, 0)


def adjoint_scratch(semaphores):
    return [
        pltpu.VMEM((BLOCKS, 2 * UVB, TILE), bf16),
        pltpu.VMEM((BLOCKS, PATCH, 2 * UVB), bf16),
        pltpu.VMEM((2, 2 * UVB, TILE), bf16),
        pltpu.SemaphoreType.DMA((semaphores,)),
    ]


def adjoint_first(ctl, metas, scaled, stacked, flipped):
    def kernel(ctl, meta0, meta1, sc0, sc1, stacked_hbm, flipped_hbm, own, pair, far, stacked, flipped, spread, sems):
        copy_s = pltpu.make_async_copy(stacked_hbm.at[:, :, :TILE], stacked, sems.at[0])
        copy_f = pltpu.make_async_copy(flipped_hbm, flipped, sems.at[1])
        copy_s.start()
        copy_f.start()

        def clear(i, c):
            at = pl.multiple_of(i * ROWS, ROWS)
            for ref in (own, pair, far):
                ref[pl.ds(at, ROWS), :] = jnp.zeros((ROWS, TILE), f32)
            return c

        lax.fori_loop(0, TILE // ROWS, clear, 0)
        copy_s.wait()
        copy_f.wait()
        near, _ = tile_steps(ctl)
        totals = (own, pair, far)
        adjoint_tile(ctl[0], 0, meta0, sc0, stacked, flipped, spread, totals)
        adjoint_tile(ctl[0], near, meta1, sc1, stacked, flipped, spread, totals)

    smem = pl.BlockSpec(memory_space=pltpu.SMEM)
    vmem = pl.BlockSpec(memory_space=pltpu.VMEM)
    hbm = pl.BlockSpec(memory_space=pl.ANY)
    return pl.pallas_call(
        kernel,
        out_shape=[jax.ShapeDtypeStruct((TILE, TILE), f32)] * 3,
        in_specs=[smem] * 3 + [vmem] * 2 + [hbm] * 2,
        out_specs=[vmem] * 3,
        scratch_shapes=adjoint_scratch(2),
        compiler_params=pltpu.CompilerParams(vmem_limit_bytes=VMEM_LIMIT),
        name="adjoint_first",
    )(ctl, *metas, *scaled, stacked, flipped)


def adjoint_last(ctl, meta, scaled, begun, stacked, flipped):
    def kernel(ctl, meta, sc, own0, pair0, far0, stacked_hbm, flipped_hbm, own, pair_out, far_out, *scratch):
        stacked, flipped, spread, sems, pair, far = scratch
        copies = [
            pltpu.make_async_copy(own0, own, sems.at[0]),
            pltpu.make_async_copy(pair0, pair, sems.at[1]),
            pltpu.make_async_copy(far0, far, sems.at[2]),
            pltpu.make_async_copy(stacked_hbm.at[:, :, :TILE], stacked, sems.at[3]),
            pltpu.make_async_copy(flipped_hbm, flipped, sems.at[4]),
        ]
        for copy in copies:
            copy.start()
        for copy in copies:
            copy.wait()
        _, outer = tile_steps(ctl)
        adjoint_tile(ctl[0], outer, meta, sc, stacked, flipped, spread, (own, pair, far))

        def emit(i, c):
            here = pl.ds(pl.multiple_of(i * ROWS, ROWS), ROWS)
            pair_out[here, :] = pair[here, :].astype(bf16)
            far_out[here, :] = far[here, :].astype(bf16)
            return c

        lax.fori_loop(0, TILE // ROWS, emit, 0)

    smem = pl.BlockSpec(memory_space=pltpu.SMEM)
    vmem = pl.BlockSpec(memory_space=pltpu.VMEM)
    hbm = pl.BlockSpec(memory_space=pl.ANY)
    return pl.pallas_call(
        kernel,
        out_shape=[
            jax.ShapeDtypeStruct((TILE, TILE), f32),
            jax.ShapeDtypeStruct((TILE, TILE), bf16),
            jax.ShapeDtypeStruct((TILE, TILE), bf16),
        ],
        in_specs=[smem] * 2 + [vmem] + [hbm] * 5,
        out_specs=[vmem] * 3,
        scratch_shapes=adjoint_scratch(5) + [pltpu.VMEM((TILE, TILE), f32)] * 2,
        compiler_params=pltpu.CompilerParams(vmem_limit_bytes=VMEM_LIMIT),
        name="adjoint_last",
    )(ctl, meta, scaled, *begun, stacked, flipped)


def mesh_moves(rows, cols):
    def pairs(move):
        made = []
        for r in range(rows):
            for c in range(cols):
                r2, c2 = move(r, c)
                if 0 <= r2 < rows and 0 <= c2 < cols:
                    made.append((r * cols + c, r2 * cols + c2))
        return made

    def outer(c):
        return c + 1 if c % 2 else c - 1

    return {
        "row_pair": pairs(lambda r, c: (r ^ 1, c)),
        "row_out": pairs(lambda r, c: (r + 2 if r % 2 else r - 2, c)),
        "row_back": pairs(lambda r, c: (r - 2 if r % 2 else r + 2, c)),
        "near": pairs(lambda r, c: (r, c ^ 1)),
        "outer": pairs(lambda r, c: (r, outer(c))),
        "row_pair_near": pairs(lambda r, c: (r ^ 1, c ^ 1)),
        "row_pair_outer": pairs(lambda r, c: (r ^ 1, outer(c))),
    }


def solution(mesh):
    moves = mesh_moves(mesh.shape["ty"], mesh.shape["tx"])
    stacked_np, flipped_np = tables()

    def send(x, what):
        return lax.ppermute(x, ("ty", "tx"), moves[what])

    def shards(sky, point_count, point_offset, beam_width, uv_bins, uv_count, uv_weight):
        stacked, flipped = jnp.asarray(stacked_np), jnp.asarray(flipped_np)
        ctl = jnp.stack([lax.axis_index("ty") % 2, lax.axis_index("tx") % 2]).astype(jnp.int32)
        meta = jnp.concatenate(
            [
                point_count.reshape(1),
                point_offset.reshape(2 * SLOTS),
                beam_width.reshape(SLOTS).astype(jnp.int32),
                uv_bins.reshape(4 * SLOTS),
                uv_count.reshape(SLOTS),
            ]
        )
        pair_sky = send(sky, "row_pair")
        far_sky = send(sky, "row_out")
        meta_own = send(meta, "row_pair")
        meta_near = send(meta, "row_pair_near")
        meta_outer = send(meta, "row_pair_outer")
        weight = send(uv_weight[0, 0], "row_pair")
        skies = (sky, pair_sky, far_sky)
        (v_outer,) = forward(("outer",), ctl, (meta_outer,), skies, stacked, flipped)
        from_outer = send(v_outer, "outer")
        v_own, v_near = forward(("own", "near"), ctl, (meta_own, meta_near), skies, stacked, flipped)
        from_near = send(v_near, "near")
        scaled = scale(meta_own, v_own, from_near, from_outer, weight)
        scaled_outer = send(scaled, "outer")
        scaled_near = send(scaled, "near")
        begun = adjoint_first(ctl, (meta_own, meta_near), (scaled, scaled_near), stacked, flipped)
        own, pair, far = adjoint_last(ctl, meta_outer, scaled_outer, begun, stacked, flipped)
        return own + send(pair, "row_pair").astype(f32) + send(far, "row_back").astype(f32)

    in_specs = (
        P("ty", "tx"),
        P("ty", "tx"),
        P("ty", "tx", None, None),
        P("ty", "tx", None),
        P("ty", "tx", None, None, None),
        P("ty", "tx", None),
        P("ty", "tx", None, None, None, None),
    )
    return jax.shard_map(shards, mesh=mesh, in_specs=in_specs, out_specs=P("ty", "tx"), check_vma=False)
```

```python
import math

import jax
import jax.numpy as jnp
import ml_dtypes
import numpy as np
from jax import lax
from jax.experimental import pallas as pl
from jax.experimental.pallas import tpu as pltpu
from jax.sharding import PartitionSpec as P

TILE = 512
PATCH = 1024
UVB = 128
BLOCKS = 8
SLOTS = 4
ROWS = 64
VMEM_LIMIT = 24 * 1024 * 1024

OFFSET, WIDTH, BINS, USED, COUNT = 0, 2, 3, 7, 8

f32 = jnp.float32
bf16 = jnp.bfloat16


def tables():
    phase = np.outer(np.arange(PATCH), np.arange(PATCH)) % PATCH
    angle = phase * (2.0 * math.pi / PATCH)
    factor = 1.0 / math.sqrt(PATCH)
    cos = (np.cos(angle) * factor).reshape(BLOCKS, UVB, PATCH)
    sin = (np.sin(angle) * factor).reshape(BLOCKS, UVB, PATCH)
    stacked = np.concatenate([cos, sin], axis=1)
    flipped = stacked.transpose(0, 2, 1)
    return stacked.astype(ml_dtypes.bfloat16), np.ascontiguousarray(flipped).astype(ml_dtypes.bfloat16)


def near_by(*arrays):
    return [pltpu.with_memory_space_constraint(x, pltpu.VMEM) for x in arrays]


def cost(pointings):
    once = 2 * 2 * UVB * TILE * (PATCH + 2 * UVB)
    return pl.CostEstimate(flops=int(1.5 * pointings * once), transcendentals=0, bytes_accessed=1 << 20)


def falloff(square, width):
    return jnp.exp(square * (-0.5 / (width * width)))


def row_factor(start, rows, oy, width):
    s = lax.broadcasted_iota(jnp.int32, (rows, 128), 0) + start
    m = ((s - oy) & (PATCH - 1)).astype(f32) - (PATCH // 2)
    return falloff(m * m, width), s


def col_factor(shift, width):
    n = lax.broadcasted_iota(jnp.int32, (8, TILE), 1) + shift
    inside = (n >= 0) & (n < PATCH)
    d = n.astype(f32) - (PATCH // 2)
    return jnp.where(inside, falloff(d * d, width), 0.0)[:1]


def twiddle(a, b, oy, shift):
    i = lax.broadcasted_iota(jnp.int32, (UVB, UVB), 0) + a * UVB
    j = lax.broadcasted_iota(jnp.int32, (UVB, UVB), 1) + b * UVB
    p = j * shift - i * oy
    quarter = (p + PATCH // 8) >> 8
    x = (p - (quarter << 8)).astype(f32) * (2.0 * math.pi / PATCH)
    y = x * x
    sin = x * (1.0 + y * (-1.0 / 6 + y * (1.0 / 120 - y * (1.0 / 5040))))
    cos = 1.0 + y * (-0.5 + y * (1.0 / 24 + y * (-1.0 / 720 + y * (1.0 / 40320))))
    odd = (quarter & 1) == 1
    c = jnp.where(odd, sin, cos)
    s = jnp.where(odd, cos, sin)
    c = jnp.where(((quarter + 1) & 2) == 2, -c, c)
    s = jnp.where((quarter & 2) == 2, -s, s)
    return c, s


def column_shift(step, ox):
    return TILE * (1 - step) - ox


def tile_steps(ctl):
    side = ctl[1]
    return 1 - 2 * side, 2 * side - 1


def lanes():
    return [slice(lane * 128, lane * 128 + 128) for lane in range(TILE // 128)]


def stage(sky, stacked, flipped):
    def kernel(*refs):
        sems = refs[6]
        copies = [pltpu.make_async_copy(refs[i], refs[3 + i], sems.at[i]) for i in range(3)]
        for copy in copies:
            copy.start()
        for copy in copies:
            copy.wait()

    arrays = (sky, stacked, flipped)
    return pl.pallas_call(
        kernel,
        out_shape=[pltpu.VMEM(x.shape, bf16) for x in arrays],
        in_specs=[pl.BlockSpec(memory_space=pltpu.HBM)] * 3,
        out_specs=[pl.BlockSpec(memory_space=pltpu.VMEM)] * 3,
        scratch_shapes=[pltpu.SemaphoreType.DMA((3,))],
        cost_estimate=pl.CostEstimate(flops=0, transcendentals=0, bytes_accessed=18 << 20),
        compiler_params=pltpu.CompilerParams(vmem_limit_bytes=VMEM_LIMIT),
        name="stage",
    )(*[pltpu.with_memory_space_constraint(x, pltpu.HBM) for x in arrays])


def forward_body(kinds, ctl, metas, sky, stacked, flipped, outs, scratch):
    own, pair, far = sky
    (window,) = scratch
    low = ctl[0]
    near, outer = tile_steps(ctl)
    steps = {"own": 0, "near": near, "outer": outer}
    for kind, meta, out in zip(kinds, metas, outs):

        def pointing(s, carry, step=steps[kind], meta=meta, out=out):
            oy, ox = meta[OFFSET, s], meta[OFFSET + 1, s]
            width = meta[WIDTH, s].astype(f32)
            shift = column_shift(step, ox)
            cols = col_factor(shift, width)

            def beam_rows(i, c):
                at = pl.multiple_of(i * ROWS, ROWS)
                here = pl.ds(at, ROWS)
                g, rows = row_factor(at, ROWS, oy, width)
                mine = jnp.where(rows >= oy, 1, 0) != low
                g2, _ = row_factor(at + TILE, ROWS, oy, width)
                there = pl.ds(pl.multiple_of(at + TILE, ROWS), ROWS)
                for part in lanes():
                    h = cols[:, part]
                    x = jnp.where(mine, own[here, part].astype(f32), far[here, part].astype(f32))
                    window[here, part] = (x * g * h).astype(bf16)
                    window[there, part] = (pair[here, part].astype(f32) * g2 * h).astype(bf16)
                return c

            lax.fori_loop(0, TILE // ROWS, beam_rows, 0)

            def uv(k, c):
                a = meta[BINS + 2 * k, s]
                b = meta[BINS + 2 * k + 1, s]
                first = jnp.dot(stacked[a], window[...], preferred_element_type=f32).astype(bf16)
                q = jnp.dot(first, flipped[b, :TILE, :], preferred_element_type=f32)
                re = q[:UVB, :UVB] - q[UVB:, UVB:]
                im = q[:UVB, UVB:] + q[UVB:, :UVB]
                cos, sin = twiddle(a, b, oy, shift)
                out[s, k, :, :UVB] = (re * cos - im * sin).astype(out.dtype)
                out[s, k, :, UVB:] = (im * cos + re * sin).astype(out.dtype)
                return c

            lax.fori_loop(0, meta[USED, s], uv, 0)
            return carry

        lax.fori_loop(0, meta[COUNT, 0], pointing, 0)


def forward(kinds, ctl, metas, sky, stacked, flipped):
    n = len(kinds)

    def kernel(ctl, *refs):
        metas, rest = refs[:n], refs[n:]
        forward_body(kinds, ctl, metas, rest[:3], rest[3], rest[4], rest[5 : 5 + n], rest[5 + n :])

    smem = pl.BlockSpec(memory_space=pltpu.SMEM)
    vmem = pl.BlockSpec(memory_space=pltpu.VMEM)
    return pl.pallas_call(
        kernel,
        out_shape=[pltpu.VMEM((SLOTS, 2, UVB, 2 * UVB), f32 if k == "own" else bf16) for k in kinds],
        in_specs=[smem] * (1 + n) + [vmem] * 5,
        out_specs=[vmem] * n,
        scratch_shapes=[pltpu.VMEM((PATCH, TILE), bf16)],
        cost_estimate=cost(3 * n - 2),
        compiler_params=pltpu.CompilerParams(vmem_limit_bytes=VMEM_LIMIT),
        name="forward_" + "_".join(kinds),
    )(ctl, *metas, *near_by(*sky), stacked, flipped)


def each_tile(meta, work):
    def pointing(s, carry):
        def uv(k, c):
            work(s, k)
            return c

        lax.fori_loop(0, meta[USED, s], uv, 0)
        return carry

    lax.fori_loop(0, meta[COUNT, 0], pointing, 0)


def add_partial(meta, mine, other):
    def kernel(meta, mine, other, out):
        def work(s, k):
            out[s, k] = mine[s, k] + other[s, k].astype(f32)

        each_tile(meta, work)

    smem = pl.BlockSpec(memory_space=pltpu.SMEM)
    vmem = pl.BlockSpec(memory_space=pltpu.VMEM)
    return pl.pallas_call(
        kernel,
        out_shape=pltpu.VMEM((SLOTS, 2, UVB, 2 * UVB), f32),
        in_specs=[smem] + [vmem] * 2,
        out_specs=vmem,
        input_output_aliases={1: 0},
        compiler_params=pltpu.CompilerParams(vmem_limit_bytes=VMEM_LIMIT),
        name="add_partial",
    )(meta, *near_by(mine, other))


def scale(meta, mine, near, weight):
    def kernel(meta, mine, near, weight, out):
        def work(s, k):
            w = weight[s, k].astype(f32)
            v = mine[s, k] + near[s, k].astype(f32)
            out[s, k, :, :UVB] = (v[:, :UVB] * w).astype(bf16)
            out[s, k, :, UVB:] = (v[:, UVB:] * w).astype(bf16)

        each_tile(meta, work)

    smem = pl.BlockSpec(memory_space=pltpu.SMEM)
    vmem = pl.BlockSpec(memory_space=pltpu.VMEM)
    return pl.pallas_call(
        kernel,
        out_shape=pltpu.VMEM((SLOTS, 2, UVB, 2 * UVB), bf16),
        in_specs=[smem] + [vmem] * 3,
        out_specs=vmem,
        compiler_params=pltpu.CompilerParams(vmem_limit_bytes=VMEM_LIMIT),
        name="scale",
    )(meta, *near_by(mine, near, weight))


def adjoint_tile(low, step, meta, scaled, stacked, flipped, spread, totals):
    own, pair, far = totals

    def pointing(s, carry):
        oy, ox = meta[OFFSET, s], meta[OFFSET + 1, s]
        width = meta[WIDTH, s].astype(f32)
        shift = column_shift(step, ox)
        cols = col_factor(shift, width)
        used = meta[USED, s]

        def uv(k, c):
            a = meta[BINS + 2 * k, s]
            b = meta[BINS + 2 * k + 1, s]
            cos, sin = twiddle(a, b, oy, shift)
            re = scaled[s, k, :, :UVB].astype(f32)
            im = scaled[s, k, :, UVB:].astype(f32)
            mr = (re * cos + im * sin).astype(bf16)
            mi = (im * cos - re * sin).astype(bf16)
            both = jnp.concatenate(
                [jnp.concatenate([mr, mi], axis=1), jnp.concatenate([mi, -mr], axis=1)], axis=0
            )
            spread[k] = jnp.dot(both, stacked[b, :, :TILE], preferred_element_type=f32).astype(bf16)
            return c

        lax.fori_loop(0, used, uv, 0)

        def add(count):
            blocks = [meta[BINS + 2 * k, s] for k in range(count)]
            big = 256

            def image(at):
                back = jnp.dot(flipped[blocks[0], pl.ds(at, big), :], spread[0], preferred_element_type=f32)
                for k in range(1, count):
                    back += jnp.dot(
                        flipped[blocks[k], pl.ds(at, big), :], spread[k], preferred_element_type=f32
                    )
                g, rows = row_factor(at, big, oy, width)
                return [back[:, part] * g * cols[:, part] for part in lanes()], rows

            def rows(i, c):
                at = pl.multiple_of(i * big, big)
                here = pl.ds(at, big)
                values, rows = image(at)
                mine = jnp.where(rows >= oy, 1, 0) != low
                for part, v in zip(lanes(), values):
                    own[here, part] = own[here, part] + jnp.where(mine, v, 0.0)
                    far[here, part] = far[here, part] + jnp.where(mine, 0.0, v)
                values, _ = image(pl.multiple_of(at + TILE, big))
                for part, v in zip(lanes(), values):
                    pair[here, part] = pair[here, part] + v
                return c

            lax.fori_loop(0, TILE // big, rows, 0)

        @pl.when(used == 1)
        def _():
            add(1)

        @pl.when(used == 2)
        def _():
            add(2)

        return carry

    lax.fori_loop(0, meta[COUNT, 0], pointing, 0)


def adjoint_first(ctl, metas, scaled, stacked, flipped):
    def kernel(ctl, meta0, meta1, sc0, sc1, stacked, flipped, own, pair, far, spread):
        def clear(i, c):
            at = pl.multiple_of(i * ROWS, ROWS)
            for ref in (own, pair, far):
                ref[pl.ds(at, ROWS), :] = jnp.zeros((ROWS, TILE), f32)
            return c

        lax.fori_loop(0, TILE // ROWS, clear, 0)
        near, _ = tile_steps(ctl)
        totals = (own, pair, far)
        adjoint_tile(ctl[0], 0, meta0, sc0, stacked, flipped, spread, totals)
        adjoint_tile(ctl[0], near, meta1, sc1, stacked, flipped, spread, totals)

    smem = pl.BlockSpec(memory_space=pltpu.SMEM)
    vmem = pl.BlockSpec(memory_space=pltpu.VMEM)
    return pl.pallas_call(
        kernel,
        out_shape=[pltpu.VMEM((TILE, TILE), f32)] * 3,
        in_specs=[smem] * 3 + [vmem] * 4,
        out_specs=[vmem] * 3,
        scratch_shapes=[pltpu.VMEM((2, 2 * UVB, TILE), bf16)],
        cost_estimate=cost(4),
        compiler_params=pltpu.CompilerParams(vmem_limit_bytes=VMEM_LIMIT),
        name="adjoint_first",
    )(ctl, *metas, *near_by(*scaled), stacked, flipped)


def adjoint_last(ctl, meta, scaled, begun, stacked, flipped):
    def kernel(ctl, meta, sc, own0, pair, far, stacked, flipped, own, pair_out, far_out, spread):
        _, outer = tile_steps(ctl)
        adjoint_tile(ctl[0], outer, meta, sc, stacked, flipped, spread, (own, pair, far))

        def emit(i, c):
            here = pl.ds(pl.multiple_of(i * ROWS, ROWS), ROWS)
            pair_out[here, :] = pair[here, :].astype(bf16)
            far_out[here, :] = far[here, :].astype(bf16)
            return c

        lax.fori_loop(0, TILE // ROWS, emit, 0)

    smem = pl.BlockSpec(memory_space=pltpu.SMEM)
    vmem = pl.BlockSpec(memory_space=pltpu.VMEM)
    return pl.pallas_call(
        kernel,
        out_shape=[
            pltpu.VMEM((TILE, TILE), f32),
            pltpu.VMEM((TILE, TILE), bf16),
            pltpu.VMEM((TILE, TILE), bf16),
        ],
        in_specs=[smem] * 2 + [vmem] * 6,
        out_specs=[vmem] * 3,
        scratch_shapes=[pltpu.VMEM((2, 2 * UVB, TILE), bf16)],
        input_output_aliases={3: 0},
        cost_estimate=cost(1),
        compiler_params=pltpu.CompilerParams(vmem_limit_bytes=VMEM_LIMIT),
        name="adjoint_last",
    )(ctl, meta, *near_by(scaled, *begun), stacked, flipped)


def mesh_moves(rows, cols):
    def pairs(move):
        made = []
        for r in range(rows):
            for c in range(cols):
                r2, c2 = move(r, c)
                if 0 <= r2 < rows and 0 <= c2 < cols:
                    made.append((r * cols + c, r2 * cols + c2))
        return made

    def outer(c):
        return c + 1 if c % 2 else c - 1

    return {
        "row_pair": pairs(lambda r, c: (r ^ 1, c)),
        "row_out": pairs(lambda r, c: (r + 2 if r % 2 else r - 2, c)),
        "row_back": pairs(lambda r, c: (r - 2 if r % 2 else r + 2, c)),
        "near": pairs(lambda r, c: (r, c ^ 1)),
        "outer": pairs(lambda r, c: (r, outer(c))),
        "row_pair_near": pairs(lambda r, c: (r ^ 1, c ^ 1)),
        "row_pair_outer": pairs(lambda r, c: (r ^ 1, outer(c))),
    }


def solution(mesh):
    moves = mesh_moves(mesh.shape["ty"], mesh.shape["tx"])
    stacked_np, flipped_np = tables()

    def send(x, what):
        return lax.ppermute(x, ("ty", "tx"), moves[what])

    def shards(sky, point_count, point_offset, beam_width, uv_bins, uv_count, uv_weight):
        ctl = jnp.stack([lax.axis_index("ty") % 2, lax.axis_index("tx") % 2]).astype(jnp.int32)
        meta = jnp.concatenate(
            [
                point_offset[0, 0].T,
                beam_width[0].astype(jnp.int32),
                uv_bins[0, 0].transpose(1, 2, 0).reshape(4, SLOTS),
                uv_count[0],
                jnp.broadcast_to(point_count, (1, SLOTS)),
            ]
        )
        pair_sky = send(sky, "row_pair")
        far_sky = send(sky, "row_out")
        meta_outer = send(meta, "row_pair_outer")
        meta_own = send(meta, "row_pair")
        meta_near = send(meta_own, "near")
        weight = send(uv_weight[0, 0], "row_pair")
        own_sky, stacked, flipped = stage(sky, jnp.asarray(stacked_np), jnp.asarray(flipped_np))
        skies = (own_sky, pair_sky, far_sky)
        (v_outer,) = forward(("outer",), ctl, (meta_outer,), skies, stacked, flipped)
        from_outer = send(v_outer, "outer")
        meta_own, meta_near, weight, v_outer = lax.optimization_barrier((meta_own, meta_near, weight, v_outer))
        v_own, v_near = forward(("own", "near"), ctl, (meta_own, meta_near), skies, stacked, flipped)
        from_near = send(v_near, "near")
        v_sum = add_partial(meta_own, v_own, from_outer)
        scaled = scale(meta_own, v_sum, from_near, weight)
        scaled_outer = send(scaled, "outer")
        scaled_near = send(scaled, "near")
        begun = adjoint_first(ctl, (meta_own, meta_near), (scaled, scaled_near), stacked, flipped)
        own, pair, far = adjoint_last(ctl, meta_outer, scaled_outer, begun, stacked, flipped)
        return own + send(pair, "row_pair").astype(f32) + send(far, "row_back").astype(f32)

    in_specs = (
        P("ty", "tx"),
        P("ty", "tx"),
        P("ty", "tx", None, None),
        P("ty", "tx", None),
        P("ty", "tx", None, None, None),
        P("ty", "tx", None),
        P("ty", "tx", None, None, None, None),
    )
    return jax.shard_map(shards, mesh=mesh, in_specs=in_specs, out_specs=P("ty", "tx"), check_vma=False)
```

```python
import math

import jax
import jax.numpy as jnp
import ml_dtypes
import numpy as np
from jax import lax
from jax.experimental import pallas as pl
from jax.experimental.pallas import tpu as pltpu
from jax.sharding import PartitionSpec as P

TILE = 512
PATCH = 1024
UVB = 128
BLOCKS = 8
SLOTS = 4
BIG = 256
ROWS = 64
VMEM_LIMIT = 24 * 1024 * 1024

OFFSET, WIDTH, BINS, USED, COUNT = 0, 2, 3, 7, 8

f32 = jnp.float32
bf16 = jnp.bfloat16


def tables():
    phase = np.outer(np.arange(PATCH), np.arange(PATCH)) % PATCH
    angle = phase * (2.0 * math.pi / PATCH)
    factor = 1.0 / math.sqrt(PATCH)
    cos = (np.cos(angle) * factor).reshape(BLOCKS, UVB, PATCH)
    sin = (np.sin(angle) * factor).reshape(BLOCKS, UVB, PATCH)
    stacked = np.concatenate([cos, sin], axis=1)
    flipped = stacked.transpose(0, 2, 1)
    return stacked.astype(ml_dtypes.bfloat16), np.ascontiguousarray(flipped).astype(ml_dtypes.bfloat16)


def near_by(*arrays):
    return [pltpu.with_memory_space_constraint(x, pltpu.VMEM) for x in arrays]


def cost(pointings):
    once = 2 * 2 * UVB * TILE * (PATCH + 2 * UVB)
    return pl.CostEstimate(flops=int(1.5 * pointings * once), transcendentals=0, bytes_accessed=1 << 20)


def falloff(square, width):
    return jnp.exp(square * (-0.5 / (width * width)))


def row_factor(start, rows, oy, width):
    s = lax.broadcasted_iota(jnp.int32, (rows, 128), 0) + start
    m = ((s - oy) & (PATCH - 1)).astype(f32) - (PATCH // 2)
    return falloff(m * m, width), s


def row_factor_in_lanes(oy, width):
    s = lax.broadcasted_iota(jnp.int32, (8, PATCH), 1)
    m = ((s - oy) & (PATCH - 1)).astype(f32) - (PATCH // 2)
    return falloff(m * m, width)[:1]


def col_factor(shift, width):
    n = lax.broadcasted_iota(jnp.int32, (8, TILE), 1) + shift
    inside = (n >= 0) & (n < PATCH)
    d = n.astype(f32) - (PATCH // 2)
    return jnp.where(inside, falloff(d * d, width), 0.0)[:1]


def twiddle(a, b, oy, shift):
    i = lax.broadcasted_iota(jnp.int32, (UVB, UVB), 0) + a * UVB
    j = lax.broadcasted_iota(jnp.int32, (UVB, UVB), 1) + b * UVB
    p = j * shift - i * oy
    quarter = (p + PATCH // 8) >> 8
    x = (p - (quarter << 8)).astype(f32) * (2.0 * math.pi / PATCH)
    y = x * x
    sin = x * (1.0 + y * (-1.0 / 6 + y * (1.0 / 120 - y * (1.0 / 5040))))
    cos = 1.0 + y * (-0.5 + y * (1.0 / 24 + y * (-1.0 / 720 + y * (1.0 / 40320))))
    odd = (quarter & 1) == 1
    c = jnp.where(odd, sin, cos)
    s = jnp.where(odd, cos, sin)
    c = jnp.where(((quarter + 1) & 2) == 2, -c, c)
    s = jnp.where((quarter & 2) == 2, -s, s)
    return c, s


def column_shift(step, ox):
    return TILE * (1 - step) - ox


def tile_steps(ctl):
    side = ctl[1]
    return 1 - 2 * side, 2 * side - 1


def lanes():
    return [slice(lane * 128, lane * 128 + 128) for lane in range(TILE // 128)]


def stage(sky, stacked, flipped):
    def kernel(*refs):
        sems = refs[6]
        copies = [pltpu.make_async_copy(refs[i], refs[3 + i], sems.at[i]) for i in range(3)]
        for copy in copies:
            copy.start()
        for copy in copies:
            copy.wait()

    arrays = (sky, stacked, flipped)
    return pl.pallas_call(
        kernel,
        out_shape=[pltpu.VMEM(x.shape, bf16) for x in arrays],
        in_specs=[pl.BlockSpec(memory_space=pltpu.HBM)] * 3,
        out_specs=[pl.BlockSpec(memory_space=pltpu.VMEM)] * 3,
        scratch_shapes=[pltpu.SemaphoreType.DMA((3,))],
        cost_estimate=pl.CostEstimate(flops=0, transcendentals=0, bytes_accessed=18 << 20),
        compiler_params=pltpu.CompilerParams(vmem_limit_bytes=VMEM_LIMIT),
        name="stage",
    )(*[pltpu.with_memory_space_constraint(x, pltpu.HBM) for x in arrays])


def forward_body(kinds, ctl, metas, sky, stacked, flipped, outs, scratch):
    own, pair, far = sky
    folded, lhs = scratch
    size = 2 * UVB
    low = ctl[0]
    near, outer = tile_steps(ctl)
    steps = {"own": 0, "near": near, "outer": outer}
    for kind, meta, out in zip(kinds, metas, outs):

        def pointing(s, carry, step=steps[kind], meta=meta, out=out):
            oy, ox = meta[OFFSET, s], meta[OFFSET + 1, s]
            width = meta[WIDTH, s].astype(f32)
            shift = column_shift(step, ox)

            def transform(count):
                bins = [(meta[BINS + 2 * k, s], meta[BINS + 2 * k + 1, s]) for k in range(count)]
                g = row_factor_in_lanes(oy, width)
                for k, (a, _) in enumerate(bins):
                    lhs[k * size : (k + 1) * size, :] = (stacked[a].astype(f32) * g).astype(bf16)
                first = jnp.dot(lhs[: count * size, TILE:], pair[...], preferred_element_type=f32)
                for at in range(0, TILE, ROWS):
                    here = slice(at, at + ROWS)
                    rows = lax.broadcasted_iota(jnp.int32, (ROWS, TILE), 0) + at
                    mine = jnp.where(rows >= oy, 1, 0) != low
                    both = jnp.where(mine, own[here, :].astype(f32), far[here, :].astype(f32))
                    folded[here, :] = both.astype(bf16)
                first += jnp.dot(lhs[: count * size, :TILE], folded[...], preferred_element_type=f32)
                first = (first * col_factor(shift, width)).astype(bf16)
                for k, (a, b) in enumerate(bins):
                    rows = first[k * size : (k + 1) * size]
                    q = jnp.dot(rows, flipped[b, :TILE, :], preferred_element_type=f32)
                    re = q[:UVB, :UVB] - q[UVB:, UVB:]
                    im = q[:UVB, UVB:] + q[UVB:, :UVB]
                    cos, sin = twiddle(a, b, oy, shift)
                    out[s, k, :, :UVB] = (re * cos - im * sin).astype(out.dtype)
                    out[s, k, :, UVB:] = (im * cos + re * sin).astype(out.dtype)

            for count in (1, 2):

                @pl.when(meta[USED, s] == count)
                def _(count=count):
                    transform(count)

            return carry

        lax.fori_loop(0, meta[COUNT, 0], pointing, 0)


def forward(kinds, ctl, metas, sky, stacked, flipped):
    n = len(kinds)

    def kernel(ctl, *refs):
        metas, rest = refs[:n], refs[n:]
        forward_body(kinds, ctl, metas, rest[:3], rest[3], rest[4], rest[5 : 5 + n], rest[5 + n :])

    smem = pl.BlockSpec(memory_space=pltpu.SMEM)
    vmem = pl.BlockSpec(memory_space=pltpu.VMEM)
    return pl.pallas_call(
        kernel,
        out_shape=[pltpu.VMEM((SLOTS, 2, UVB, 2 * UVB), f32 if k == "own" else bf16) for k in kinds],
        in_specs=[smem] * (1 + n) + [vmem] * 5,
        out_specs=[vmem] * n,
        scratch_shapes=[
            pltpu.VMEM((TILE, TILE), bf16),
            pltpu.VMEM((4 * UVB, PATCH), bf16),
        ],
        cost_estimate=cost(3 * n - 2),
        compiler_params=pltpu.CompilerParams(vmem_limit_bytes=VMEM_LIMIT),
        name="forward_" + "_".join(kinds),
    )(ctl, *metas, *near_by(*sky), stacked, flipped)


def each_tile(meta, work):
    def pointing(s, carry):
        def uv(k, c):
            work(s, k)
            return c

        lax.fori_loop(0, meta[USED, s], uv, 0)
        return carry

    lax.fori_loop(0, meta[COUNT, 0], pointing, 0)


def add_partial(meta, mine, other):
    def kernel(meta, mine, other, out):
        def work(s, k):
            out[s, k] = mine[s, k] + other[s, k].astype(f32)

        each_tile(meta, work)

    smem = pl.BlockSpec(memory_space=pltpu.SMEM)
    vmem = pl.BlockSpec(memory_space=pltpu.VMEM)
    return pl.pallas_call(
        kernel,
        out_shape=pltpu.VMEM((SLOTS, 2, UVB, 2 * UVB), f32),
        in_specs=[smem] + [vmem] * 2,
        out_specs=vmem,
        input_output_aliases={1: 0},
        compiler_params=pltpu.CompilerParams(vmem_limit_bytes=VMEM_LIMIT),
        name="add_partial",
    )(meta, *near_by(mine, other))


def scale(meta, mine, near, weight):
    def kernel(meta, mine, near, weight, out):
        def work(s, k):
            w = weight[s, k].astype(f32)
            v = mine[s, k] + near[s, k].astype(f32)
            out[s, k, :, :UVB] = (v[:, :UVB] * w).astype(bf16)
            out[s, k, :, UVB:] = (v[:, UVB:] * w).astype(bf16)

        each_tile(meta, work)

    smem = pl.BlockSpec(memory_space=pltpu.SMEM)
    vmem = pl.BlockSpec(memory_space=pltpu.VMEM)
    return pl.pallas_call(
        kernel,
        out_shape=pltpu.VMEM((SLOTS, 2, UVB, 2 * UVB), bf16),
        in_specs=[smem] + [vmem] * 3,
        out_specs=vmem,
        compiler_params=pltpu.CompilerParams(vmem_limit_bytes=VMEM_LIMIT),
        name="scale",
    )(meta, *near_by(mine, near, weight))


def adjoint_tile(low, step, meta, scaled, stacked, flipped, spread, totals):
    own, pair, far = totals

    def pointing(s, carry):
        oy, ox = meta[OFFSET, s], meta[OFFSET + 1, s]
        width = meta[WIDTH, s].astype(f32)
        shift = column_shift(step, ox)

        def transform(count):
            bins = [(meta[BINS + 2 * k, s], meta[BINS + 2 * k + 1, s]) for k in range(count)]
            h = col_factor(shift, width)
            for k, (a, b) in enumerate(bins):
                cos, sin = twiddle(a, b, oy, shift)
                re = scaled[s, k, :, :UVB].astype(f32)
                im = scaled[s, k, :, UVB:].astype(f32)
                mr = (re * cos + im * sin).astype(bf16)
                mi = (im * cos - re * sin).astype(bf16)
                both = jnp.concatenate(
                    [jnp.concatenate([mr, mi], axis=1), jnp.concatenate([mi, -mr], axis=1)], axis=0
                )
                value = jnp.dot(both, stacked[b, :, :TILE], preferred_element_type=f32)
                spread[k] = (value * h).astype(bf16)

            def image(at):
                here = slice(at, at + BIG)
                back = jnp.dot(flipped[bins[0][0], here, :], spread[0], preferred_element_type=f32)
                for k in range(1, count):
                    back += jnp.dot(flipped[bins[k][0], here, :], spread[k], preferred_element_type=f32)
                g, rows = row_factor(at, BIG, oy, width)
                return [back[:, part] * g for part in lanes()], rows

            for at in range(0, TILE, BIG):
                here = slice(at, at + BIG)
                values, _ = image(at + TILE)
                for part, v in zip(lanes(), values):
                    pair[here, part] = pair[here, part] + v
                values, rows = image(at)
                mine = jnp.where(rows >= oy, 1, 0) != low
                for part, v in zip(lanes(), values):
                    own[here, part] = own[here, part] + jnp.where(mine, v, 0.0)
                    far[here, part] = far[here, part] + jnp.where(mine, 0.0, v)

        for count in (1, 2):

            @pl.when(meta[USED, s] == count)
            def _(count=count):
                transform(count)

        return carry

    lax.fori_loop(0, meta[COUNT, 0], pointing, 0)


def adjoint_first(ctl, metas, scaled, stacked, flipped):
    def kernel(ctl, meta0, meta1, sc0, sc1, stacked, flipped, own, pair, far, spread):
        def clear(i, c):
            at = pl.multiple_of(i * ROWS, ROWS)
            for ref in (own, pair, far):
                ref[pl.ds(at, ROWS), :] = jnp.zeros((ROWS, TILE), f32)
            return c

        lax.fori_loop(0, TILE // ROWS, clear, 0)
        near, _ = tile_steps(ctl)
        totals = (own, pair, far)
        adjoint_tile(ctl[0], 0, meta0, sc0, stacked, flipped, spread, totals)
        adjoint_tile(ctl[0], near, meta1, sc1, stacked, flipped, spread, totals)

    smem = pl.BlockSpec(memory_space=pltpu.SMEM)
    vmem = pl.BlockSpec(memory_space=pltpu.VMEM)
    return pl.pallas_call(
        kernel,
        out_shape=[pltpu.VMEM((TILE, TILE), f32)] * 3,
        in_specs=[smem] * 3 + [vmem] * 4,
        out_specs=[vmem] * 3,
        scratch_shapes=[pltpu.VMEM((2, 2 * UVB, TILE), bf16)],
        cost_estimate=cost(4),
        compiler_params=pltpu.CompilerParams(vmem_limit_bytes=VMEM_LIMIT),
        name="adjoint_first",
    )(ctl, *metas, *near_by(*scaled), stacked, flipped)


def adjoint_last(ctl, meta, scaled, begun, stacked, flipped):
    def kernel(ctl, meta, sc, own0, pair, far, stacked, flipped, own, pair_out, far_out, spread):
        _, outer = tile_steps(ctl)
        adjoint_tile(ctl[0], outer, meta, sc, stacked, flipped, spread, (own, pair, far))

        def emit(i, c):
            here = pl.ds(pl.multiple_of(i * ROWS, ROWS), ROWS)
            pair_out[here, :] = pair[here, :].astype(bf16)
            far_out[here, :] = far[here, :].astype(bf16)
            return c

        lax.fori_loop(0, TILE // ROWS, emit, 0)

    smem = pl.BlockSpec(memory_space=pltpu.SMEM)
    vmem = pl.BlockSpec(memory_space=pltpu.VMEM)
    return pl.pallas_call(
        kernel,
        out_shape=[
            pltpu.VMEM((TILE, TILE), f32),
            pltpu.VMEM((TILE, TILE), bf16),
            pltpu.VMEM((TILE, TILE), bf16),
        ],
        in_specs=[smem] * 2 + [vmem] * 6,
        out_specs=[vmem] * 3,
        scratch_shapes=[pltpu.VMEM((2, 2 * UVB, TILE), bf16)],
        input_output_aliases={3: 0},
        cost_estimate=cost(1),
        compiler_params=pltpu.CompilerParams(vmem_limit_bytes=VMEM_LIMIT),
        name="adjoint_last",
    )(ctl, meta, *near_by(scaled, *begun), stacked, flipped)


def mesh_moves(rows, cols):
    def pairs(move):
        made = []
        for r in range(rows):
            for c in range(cols):
                r2, c2 = move(r, c)
                if 0 <= r2 < rows and 0 <= c2 < cols:
                    made.append((r * cols + c, r2 * cols + c2))
        return made

    def outer(c):
        return c + 1 if c % 2 else c - 1

    return {
        "row_pair": pairs(lambda r, c: (r ^ 1, c)),
        "row_out": pairs(lambda r, c: (r + 2 if r % 2 else r - 2, c)),
        "row_back": pairs(lambda r, c: (r - 2 if r % 2 else r + 2, c)),
        "near": pairs(lambda r, c: (r, c ^ 1)),
        "outer": pairs(lambda r, c: (r, outer(c))),
        "row_pair_near": pairs(lambda r, c: (r ^ 1, c ^ 1)),
        "row_pair_outer": pairs(lambda r, c: (r ^ 1, outer(c))),
    }


def solution(mesh):
    moves = mesh_moves(mesh.shape["ty"], mesh.shape["tx"])
    stacked_np, flipped_np = tables()

    def send(x, what):
        return lax.ppermute(x, ("ty", "tx"), moves[what])

    def shards(sky, point_count, point_offset, beam_width, uv_bins, uv_count, uv_weight):
        ctl = jnp.stack([lax.axis_index("ty") % 2, lax.axis_index("tx") % 2]).astype(jnp.int32)
        meta = jnp.concatenate(
            [
                point_offset[0, 0].T,
                beam_width[0].astype(jnp.int32),
                uv_bins[0, 0].transpose(1, 2, 0).reshape(4, SLOTS),
                uv_count[0],
                jnp.broadcast_to(point_count, (1, SLOTS)),
            ]
        )
        pair_sky = send(sky, "row_pair")
        far_sky = send(sky, "row_out")
        meta_outer = send(meta, "row_pair_outer")
        meta_own = send(meta, "row_pair")
        meta_near = send(meta_own, "near")
        held, meta_outer, meta_own = lax.optimization_barrier((uv_weight[0, 0], meta_outer, meta_own))
        weight = send(held, "row_pair")
        own_sky, stacked, flipped = stage(sky, jnp.asarray(stacked_np), jnp.asarray(flipped_np))
        skies = (own_sky, pair_sky, far_sky)
        (v_outer,) = forward(("outer",), ctl, (meta_outer,), skies, stacked, flipped)
        from_outer = send(v_outer, "outer")
        meta_own, meta_near, weight, v_outer = lax.optimization_barrier((meta_own, meta_near, weight, v_outer))
        v_own, v_near = forward(("own", "near"), ctl, (meta_own, meta_near), skies, stacked, flipped)
        from_near = send(v_near, "near")
        v_sum = add_partial(meta_own, v_own, from_outer)
        scaled = scale(meta_own, v_sum, from_near, weight)
        scaled_outer = send(scaled, "outer")
        scaled_near = send(scaled, "near")
        begun = adjoint_first(ctl, (meta_own, meta_near), (scaled, scaled_near), stacked, flipped)
        own, pair, far = adjoint_last(ctl, meta_outer, scaled_outer, begun, stacked, flipped)
        return own + send(pair, "row_pair").astype(f32) + send(far, "row_back").astype(f32)

    in_specs = (
        P("ty", "tx"),
        P("ty", "tx"),
        P("ty", "tx", None, None),
        P("ty", "tx", None),
        P("ty", "tx", None, None, None),
        P("ty", "tx", None),
        P("ty", "tx", None, None, None, None),
    )
    return jax.shard_map(shards, mesh=mesh, in_specs=in_specs, out_specs=P("ty", "tx"), check_vma=False)
```

```python
import math

import jax
import jax.numpy as jnp
import ml_dtypes
import numpy as np
from jax import lax
from jax.experimental import pallas as pl
from jax.experimental.pallas import tpu as pltpu
from jax.sharding import PartitionSpec as P

TILE = 512
PATCH = 1024
UVB = 128
BLOCKS = 8
SLOTS = 4
BIG = 256
ROWS = 64
VMEM_LIMIT = 24 * 1024 * 1024

OFFSET, WIDTH, BINS, USED, COUNT = 0, 2, 3, 7, 8

f32 = jnp.float32
bf16 = jnp.bfloat16


def tables():
    phase = np.outer(np.arange(PATCH), np.arange(PATCH)) % PATCH
    angle = phase * (2.0 * math.pi / PATCH)
    factor = 1.0 / math.sqrt(PATCH)
    cos = (np.cos(angle) * factor).reshape(BLOCKS, UVB, PATCH)
    sin = (np.sin(angle) * factor).reshape(BLOCKS, UVB, PATCH)
    stacked = np.concatenate([cos, sin], axis=1)
    stacked = stacked[:, :, :TILE]
    flipped = stacked.transpose(0, 2, 1)
    return stacked.astype(ml_dtypes.bfloat16), np.ascontiguousarray(flipped).astype(ml_dtypes.bfloat16)


def near_by(*arrays):
    return [pltpu.with_memory_space_constraint(x, pltpu.VMEM) for x in arrays]


def cost(pointings):
    once = 2 * 2 * UVB * TILE * (PATCH + 2 * UVB)
    return pl.CostEstimate(flops=int(1.5 * pointings * once), transcendentals=0, bytes_accessed=1 << 20)


def falloff(square, width):
    return jnp.exp(square * (-0.5 / (width * width)))


def row_factor(start, rows, oy, width):
    s = lax.broadcasted_iota(jnp.int32, (rows, 128), 0) + start
    m = ((s - oy) & (PATCH - 1)).astype(f32) - (PATCH // 2)
    return falloff(m * m, width), s


def row_factor_in_lanes(oy, width):
    s = lax.broadcasted_iota(jnp.int32, (8, PATCH), 1)
    m = ((s - oy) & (PATCH - 1)).astype(f32) - (PATCH // 2)
    return falloff(m * m, width)


def alternating():
    i = lax.broadcasted_iota(jnp.int32, (8, TILE), 0)
    return jnp.where((i & 1) == 1, -1.0, 1.0).astype(f32)


def times_rows(x, factor):
    return (x.reshape(x.shape[0] // 8, 8, x.shape[1]) * factor[None]).reshape(x.shape)


def col_factor(shift, width):
    n = lax.broadcasted_iota(jnp.int32, (8, TILE), 1) + shift
    inside = (n >= 0) & (n < PATCH)
    d = n.astype(f32) - (PATCH // 2)
    return jnp.where(inside, falloff(d * d, width), 0.0)


def twiddle(a, b, oy, shift):
    i = lax.broadcasted_iota(jnp.int32, (UVB, UVB), 0) + a * UVB
    j = lax.broadcasted_iota(jnp.int32, (UVB, UVB), 1) + b * UVB
    p = j * shift - i * oy
    quarter = (p + PATCH // 8) >> 8
    x = (p - (quarter << 8)).astype(f32) * (2.0 * math.pi / PATCH)
    y = x * x
    sin = x * (1.0 + y * (-1.0 / 6 + y * (1.0 / 120 - y * (1.0 / 5040))))
    cos = 1.0 + y * (-0.5 + y * (1.0 / 24 + y * (-1.0 / 720 + y * (1.0 / 40320))))
    odd = (quarter & 1) == 1
    c = jnp.where(odd, sin, cos)
    s = jnp.where(odd, cos, sin)
    c = jnp.where(((quarter + 1) & 2) == 2, -c, c)
    s = jnp.where((quarter & 2) == 2, -s, s)
    return c, s


def column_shift(step, ox):
    return TILE * (1 - step) - ox


def tile_steps(ctl):
    side = ctl[1]
    return 1 - 2 * side, 2 * side - 1


def lanes():
    return [slice(lane * 128, lane * 128 + 128) for lane in range(TILE // 128)]


def stage(sky, stacked, flipped):
    def kernel(*refs):
        sems = refs[6]
        copies = [pltpu.make_async_copy(refs[i], refs[3 + i], sems.at[i]) for i in range(3)]
        for copy in copies:
            copy.start()
        for copy in copies:
            copy.wait()

    arrays = (sky, stacked, flipped)
    return pl.pallas_call(
        kernel,
        out_shape=[pltpu.VMEM(x.shape, bf16) for x in arrays],
        in_specs=[pl.BlockSpec(memory_space=pltpu.HBM)] * 3,
        out_specs=[pl.BlockSpec(memory_space=pltpu.VMEM)] * 3,
        scratch_shapes=[pltpu.SemaphoreType.DMA((3,))],
        cost_estimate=pl.CostEstimate(flops=0, transcendentals=0, bytes_accessed=18 << 20),
        compiler_params=pltpu.CompilerParams(vmem_limit_bytes=VMEM_LIMIT),
        name="stage",
    )(*[pltpu.with_memory_space_constraint(x, pltpu.HBM) for x in arrays])


def forward_body(kinds, ctl, metas, sky, stacked, flipped, outs, scratch):
    own, pair, far = sky
    folded, lhs = scratch
    size = 2 * UVB
    low = ctl[0]
    near, outer = tile_steps(ctl)
    steps = {"own": 0, "near": near, "outer": outer}
    for kind, meta, out in zip(kinds, metas, outs):

        def pointing(s, carry, step=steps[kind], meta=meta, out=out):
            oy, ox = meta[OFFSET, s], meta[OFFSET + 1, s]
            width = meta[WIDTH, s].astype(f32)
            shift = column_shift(step, ox)

            def transform(count):
                bins = [(meta[BINS + 2 * k, s], meta[BINS + 2 * k + 1, s]) for k in range(count)]
                g = row_factor_in_lanes(oy, width)
                for k, (a, _) in enumerate(bins):
                    rows = slice(k * size, (k + 1) * size)
                    table = stacked[a].astype(f32)
                    lhs[rows, TILE:] = times_rows(table, g[:, TILE:] * alternating()).astype(bf16)
                    lhs[rows, :TILE] = times_rows(table, g[:, :TILE]).astype(bf16)
                first = jnp.dot(lhs[: count * size, TILE:], pair[...], preferred_element_type=f32)
                for at in range(0, TILE, ROWS):
                    here = slice(at, at + ROWS)
                    rows = lax.broadcasted_iota(jnp.int32, (ROWS, TILE), 0) + at
                    mine = jnp.where(rows >= oy, 1, 0) != low
                    both = jnp.where(mine, own[here, :].astype(f32), far[here, :].astype(f32))
                    folded[here, :] = both.astype(bf16)
                first += jnp.dot(lhs[: count * size, :TILE], folded[...], preferred_element_type=f32)
                first = times_rows(first, col_factor(shift, width)).astype(bf16)
                for k, (a, b) in enumerate(bins):
                    rows = first[k * size : (k + 1) * size]
                    q = jnp.dot(rows, flipped[b], preferred_element_type=f32)
                    re = q[:UVB, :UVB] - q[UVB:, UVB:]
                    im = q[:UVB, UVB:] + q[UVB:, :UVB]
                    cos, sin = twiddle(a, b, oy, shift)
                    out[s, k, :, :UVB] = (re * cos - im * sin).astype(out.dtype)
                    out[s, k, :, UVB:] = (im * cos + re * sin).astype(out.dtype)

            for count in (1, 2):

                @pl.when(meta[USED, s] == count)
                def _(count=count):
                    transform(count)

            return carry

        lax.fori_loop(0, meta[COUNT, 0], pointing, 0)


def forward(kinds, ctl, metas, sky, stacked, flipped):
    n = len(kinds)

    def kernel(ctl, *refs):
        metas, rest = refs[:n], refs[n:]
        forward_body(kinds, ctl, metas, rest[:3], rest[3], rest[4], rest[5 : 5 + n], rest[5 + n :])

    smem = pl.BlockSpec(memory_space=pltpu.SMEM)
    vmem = pl.BlockSpec(memory_space=pltpu.VMEM)
    return pl.pallas_call(
        kernel,
        out_shape=[pltpu.VMEM((SLOTS, 2, UVB, 2 * UVB), f32 if k == "own" else bf16) for k in kinds],
        in_specs=[smem] * (1 + n) + [vmem] * 5,
        out_specs=[vmem] * n,
        scratch_shapes=[
            pltpu.VMEM((TILE, TILE), bf16),
            pltpu.VMEM((4 * UVB, PATCH), bf16),
        ],
        cost_estimate=cost(3 * n - 2),
        compiler_params=pltpu.CompilerParams(vmem_limit_bytes=VMEM_LIMIT),
        name="forward_" + "_".join(kinds),
    )(ctl, *metas, *near_by(*sky), stacked, flipped)


def each_tile(meta, work):
    def pointing(s, carry):
        def uv(k, c):
            work(s, k)
            return c

        lax.fori_loop(0, meta[USED, s], uv, 0)
        return carry

    lax.fori_loop(0, meta[COUNT, 0], pointing, 0)


def add_partial(meta, mine, other):
    def kernel(meta, mine, other, out):
        def work(s, k):
            out[s, k] = mine[s, k] + other[s, k].astype(f32)

        each_tile(meta, work)

    smem = pl.BlockSpec(memory_space=pltpu.SMEM)
    vmem = pl.BlockSpec(memory_space=pltpu.VMEM)
    return pl.pallas_call(
        kernel,
        out_shape=pltpu.VMEM((SLOTS, 2, UVB, 2 * UVB), f32),
        in_specs=[smem] + [vmem] * 2,
        out_specs=vmem,
        input_output_aliases={1: 0},
        compiler_params=pltpu.CompilerParams(vmem_limit_bytes=VMEM_LIMIT),
        name="add_partial",
    )(meta, *near_by(mine, other))


def scale(meta, mine, near, weight):
    def kernel(meta, mine, near, weight, out):
        def work(s, k):
            w = weight[s, k].astype(f32)
            v = mine[s, k] + near[s, k].astype(f32)
            out[s, k, :, :UVB] = (v[:, :UVB] * w).astype(bf16)
            out[s, k, :, UVB:] = (v[:, UVB:] * w).astype(bf16)

        each_tile(meta, work)

    smem = pl.BlockSpec(memory_space=pltpu.SMEM)
    vmem = pl.BlockSpec(memory_space=pltpu.VMEM)
    return pl.pallas_call(
        kernel,
        out_shape=pltpu.VMEM((SLOTS, 2, UVB, 2 * UVB), bf16),
        in_specs=[smem] + [vmem] * 3,
        out_specs=vmem,
        compiler_params=pltpu.CompilerParams(vmem_limit_bytes=VMEM_LIMIT),
        name="scale",
    )(meta, *near_by(mine, near, weight))


def adjoint_tile(low, step, meta, scaled, stacked, flipped, spread, totals):
    own, pair, far = totals

    def pointing(s, carry):
        oy, ox = meta[OFFSET, s], meta[OFFSET + 1, s]
        width = meta[WIDTH, s].astype(f32)
        shift = column_shift(step, ox)

        def transform(count):
            bins = [(meta[BINS + 2 * k, s], meta[BINS + 2 * k + 1, s]) for k in range(count)]
            h = col_factor(shift, width)
            for k, (a, b) in enumerate(bins):
                cos, sin = twiddle(a, b, oy, shift)
                re = scaled[s, k, :, :UVB].astype(f32)
                im = scaled[s, k, :, UVB:].astype(f32)
                mr = (re * cos + im * sin).astype(bf16)
                mi = (im * cos - re * sin).astype(bf16)
                both = jnp.concatenate(
                    [jnp.concatenate([mr, mi], axis=1), jnp.concatenate([mi, -mr], axis=1)], axis=0
                )
                value = jnp.dot(both, stacked[b], preferred_element_type=f32)
                spread[0, k] = times_rows(value, h).astype(bf16)
                spread[1, k] = times_rows(value, h * alternating()).astype(bf16)

            def image(at, upper):
                here = slice(at, at + BIG)
                back = jnp.dot(flipped[bins[0][0], here, :], spread[upper, 0], preferred_element_type=f32)
                for k in range(1, count):
                    back += jnp.dot(flipped[bins[k][0], here, :], spread[upper, k], preferred_element_type=f32)
                g, rows = row_factor(at + upper * TILE, BIG, oy, width)
                return [back[:, part] * g for part in lanes()], rows

            for at in range(0, TILE, BIG):
                here = slice(at, at + BIG)
                values, _ = image(at, 1)
                for part, v in zip(lanes(), values):
                    pair[here, part] = pair[here, part] + v
                values, rows = image(at, 0)
                mine = jnp.where(rows >= oy, 1, 0) != low
                for part, v in zip(lanes(), values):
                    own[here, part] = own[here, part] + jnp.where(mine, v, 0.0)
                    far[here, part] = far[here, part] + jnp.where(mine, 0.0, v)

        for count in (1, 2):

            @pl.when(meta[USED, s] == count)
            def _(count=count):
                transform(count)

        return carry

    lax.fori_loop(0, meta[COUNT, 0], pointing, 0)


def adjoint_own(ctl, meta, scaled, stacked, flipped):
    def kernel(ctl, meta, sc, stacked, flipped, own, pair, far, spread):
        def clear(i, c):
            at = pl.multiple_of(i * ROWS, ROWS)
            for ref in (own, pair, far):
                ref[pl.ds(at, ROWS), :] = jnp.zeros((ROWS, TILE), f32)
            return c

        lax.fori_loop(0, TILE // ROWS, clear, 0)
        adjoint_tile(ctl[0], 0, meta, sc, stacked, flipped, spread, (own, pair, far))

    smem = pl.BlockSpec(memory_space=pltpu.SMEM)
    vmem = pl.BlockSpec(memory_space=pltpu.VMEM)
    return pl.pallas_call(
        kernel,
        out_shape=[pltpu.VMEM((TILE, TILE), f32)] * 3,
        in_specs=[smem] * 2 + [vmem] * 3,
        out_specs=[vmem] * 3,
        scratch_shapes=[pltpu.VMEM((2, 2, 2 * UVB, TILE), bf16)],
        cost_estimate=cost(2),
        compiler_params=pltpu.CompilerParams(vmem_limit_bytes=VMEM_LIMIT),
        name="adjoint_own",
    )(ctl, meta, *near_by(scaled), stacked, flipped)


def adjoint_near(ctl, meta, scaled, begun, stacked, flipped):
    def kernel(ctl, meta, sc, own0, pair0, far0, stacked, flipped, own, pair, far, spread):
        near, _ = tile_steps(ctl)
        adjoint_tile(ctl[0], near, meta, sc, stacked, flipped, spread, (own, pair, far))

    smem = pl.BlockSpec(memory_space=pltpu.SMEM)
    vmem = pl.BlockSpec(memory_space=pltpu.VMEM)
    return pl.pallas_call(
        kernel,
        out_shape=[pltpu.VMEM((TILE, TILE), f32)] * 3,
        in_specs=[smem] * 2 + [vmem] * 6,
        out_specs=[vmem] * 3,
        scratch_shapes=[pltpu.VMEM((2, 2, 2 * UVB, TILE), bf16)],
        input_output_aliases={3: 0, 4: 1, 5: 2},
        cost_estimate=cost(2),
        compiler_params=pltpu.CompilerParams(vmem_limit_bytes=VMEM_LIMIT),
        name="adjoint_near",
    )(ctl, meta, *near_by(scaled, *begun), stacked, flipped)


def adjoint_last(ctl, meta, scaled, begun, stacked, flipped):
    def kernel(ctl, meta, sc, own0, pair, far, stacked, flipped, own, pair_out, far_out, spread):
        _, outer = tile_steps(ctl)
        adjoint_tile(ctl[0], outer, meta, sc, stacked, flipped, spread, (own, pair, far))

        def emit(i, c):
            here = pl.ds(pl.multiple_of(i * ROWS, ROWS), ROWS)
            pair_out[here, :] = pair[here, :].astype(bf16)
            far_out[here, :] = far[here, :].astype(bf16)
            return c

        lax.fori_loop(0, TILE // ROWS, emit, 0)

    smem = pl.BlockSpec(memory_space=pltpu.SMEM)
    vmem = pl.BlockSpec(memory_space=pltpu.VMEM)
    return pl.pallas_call(
        kernel,
        out_shape=[
            pltpu.VMEM((TILE, TILE), f32),
            pltpu.VMEM((TILE, TILE), bf16),
            pltpu.VMEM((TILE, TILE), bf16),
        ],
        in_specs=[smem] * 2 + [vmem] * 6,
        out_specs=[vmem] * 3,
        scratch_shapes=[pltpu.VMEM((2, 2, 2 * UVB, TILE), bf16)],
        input_output_aliases={3: 0},
        cost_estimate=cost(1),
        compiler_params=pltpu.CompilerParams(vmem_limit_bytes=VMEM_LIMIT),
        name="adjoint_last",
    )(ctl, meta, *near_by(scaled, *begun), stacked, flipped)


def mesh_moves(rows, cols):
    def pairs(move):
        made = []
        for r in range(rows):
            for c in range(cols):
                r2, c2 = move(r, c)
                if 0 <= r2 < rows and 0 <= c2 < cols:
                    made.append((r * cols + c, r2 * cols + c2))
        return made

    def outer(c):
        return c + 1 if c % 2 else c - 1

    return {
        "row_pair": pairs(lambda r, c: (r ^ 1, c)),
        "row_out": pairs(lambda r, c: (r + 2 if r % 2 else r - 2, c)),
        "row_back": pairs(lambda r, c: (r - 2 if r % 2 else r + 2, c)),
        "near": pairs(lambda r, c: (r, c ^ 1)),
        "outer": pairs(lambda r, c: (r, outer(c))),
        "row_pair_near": pairs(lambda r, c: (r ^ 1, c ^ 1)),
        "row_pair_outer": pairs(lambda r, c: (r ^ 1, outer(c))),
    }


def solution(mesh):
    moves = mesh_moves(mesh.shape["ty"], mesh.shape["tx"])
    stacked_np, flipped_np = tables()

    def send(x, what):
        return lax.ppermute(x, ("ty", "tx"), moves[what])

    def shards(sky, point_count, point_offset, beam_width, uv_bins, uv_count, uv_weight):
        ctl = jnp.stack([lax.axis_index("ty") % 2, lax.axis_index("tx") % 2]).astype(jnp.int32)
        rows = (
            (OFFSET, point_offset[0, 0].T),
            (WIDTH, beam_width[0].astype(jnp.int32)),
            (BINS, uv_bins[0, 0].transpose(1, 2, 0).reshape(4, SLOTS)),
            (USED, uv_count[0]),
            (COUNT, jnp.broadcast_to(point_count, (1, SLOTS))),
        )
        meta = sum(jnp.pad(x, ((at, COUNT + 1 - at - x.shape[0]), (0, 0))) for at, x in rows)
        pair_sky = send(sky, "row_pair")
        far_sky = send(sky, "row_out")
        meta_outer = send(meta, "row_pair_outer")
        meta_own = send(meta, "row_pair")
        meta_near = send(meta, "row_pair_near")
        own_sky, stacked, flipped = stage(sky, jnp.asarray(stacked_np), jnp.asarray(flipped_np))
        weight = send(uv_weight[0, 0], "row_pair")
        skies = (own_sky, pair_sky, far_sky)
        (v_outer,) = forward(("outer",), ctl, (meta_outer,), skies, stacked, flipped)
        from_outer = send(v_outer, "outer")
        meta_own, meta_near, weight, v_outer = lax.optimization_barrier((meta_own, meta_near, weight, v_outer))
        v_own, v_near = forward(("own", "near"), ctl, (meta_own, meta_near), skies, stacked, flipped)
        from_near = send(v_near, "near")
        v_sum = add_partial(meta_own, v_own, from_outer)
        scaled = scale(meta_own, v_sum, from_near, weight)
        scaled_outer = send(scaled, "outer")
        scaled_near = send(scaled, "near")
        begun = adjoint_own(ctl, meta_own, scaled, stacked, flipped)
        begun = adjoint_near(ctl, meta_near, scaled_near, begun, stacked, flipped)
        own, pair, far = adjoint_last(ctl, meta_outer, scaled_outer, begun, stacked, flipped)
        return own + send(pair, "row_pair").astype(f32) + send(far, "row_back").astype(f32)

    in_specs = (
        P("ty", "tx"),
        P("ty", "tx"),
        P("ty", "tx", None, None),
        P("ty", "tx", None),
        P("ty", "tx", None, None, None),
        P("ty", "tx", None),
        P("ty", "tx", None, None, None, None),
    )
    return jax.shard_map(shards, mesh=mesh, in_specs=in_specs, out_specs=P("ty", "tx"), check_vma=False)
```

```python
import math

import jax
import jax.numpy as jnp
import ml_dtypes
import numpy as np
from jax import lax
from jax.experimental import pallas as pl
from jax.experimental.pallas import tpu as pltpu
from jax.sharding import PartitionSpec as P

TILE = 512
PATCH = 1024
UVB = 128
BLOCKS = 8
SLOTS = 4
CHUNK = 2
BIG = 256
ROWS = 64
VMEM_LIMIT = 24 * 1024 * 1024

OFFSET, WIDTH, BINS, USED, COUNT = 0, 2, 3, 7, 8

f32 = jnp.float32
bf16 = jnp.bfloat16


def tables():
    phase = np.outer(np.arange(PATCH), np.arange(PATCH)) % PATCH
    angle = phase * (2.0 * math.pi / PATCH)
    factor = 1.0 / math.sqrt(PATCH)
    cos = (np.cos(angle) * factor).reshape(BLOCKS, UVB, PATCH)
    sin = (np.sin(angle) * factor).reshape(BLOCKS, UVB, PATCH)
    stacked = np.concatenate([cos, sin], axis=1)
    stacked = stacked[:, :, :TILE]
    flipped = stacked.transpose(0, 2, 1)
    return stacked.astype(ml_dtypes.bfloat16), np.ascontiguousarray(flipped).astype(ml_dtypes.bfloat16)


def near_by(*arrays):
    return [pltpu.with_memory_space_constraint(x, pltpu.VMEM) for x in arrays]


def cost(pointings):
    once = 2 * 2 * UVB * TILE * (PATCH + 2 * UVB)
    return pl.CostEstimate(flops=int(1.5 * pointings * once), transcendentals=0, bytes_accessed=1 << 20)


def falloff(square, width):
    return jnp.exp(square * (-0.5 / (width * width)))


def row_factor(start, rows, oy, width):
    s = lax.broadcasted_iota(jnp.int32, (rows, 128), 0) + start
    m = ((s - oy) & (PATCH - 1)).astype(f32) - (PATCH // 2)
    return falloff(m * m, width), s


def row_factor_in_lanes(oy, width):
    s = lax.broadcasted_iota(jnp.int32, (8, PATCH), 1)
    m = ((s - oy) & (PATCH - 1)).astype(f32) - (PATCH // 2)
    return falloff(m * m, width)


def alternating():
    i = lax.broadcasted_iota(jnp.int32, (8, TILE), 0)
    return jnp.where((i & 1) == 1, -1.0, 1.0).astype(f32)


def times_rows(x, factor):
    return (x.reshape(x.shape[0] // 8, 8, x.shape[1]) * factor[None]).reshape(x.shape)


def col_factor(shift, width):
    n = lax.broadcasted_iota(jnp.int32, (8, TILE), 1) + shift
    inside = (n >= 0) & (n < PATCH)
    d = n.astype(f32) - (PATCH // 2)
    return jnp.where(inside, falloff(d * d, width), 0.0)


def twiddle(a, b, oy, shift):
    i = lax.broadcasted_iota(jnp.int32, (UVB, UVB), 0) + a * UVB
    j = lax.broadcasted_iota(jnp.int32, (UVB, UVB), 1) + b * UVB
    p = j * shift - i * oy
    quarter = (p + PATCH // 8) >> 8
    x = (p - (quarter << 8)).astype(f32) * (2.0 * math.pi / PATCH)
    y = x * x
    sin = x * (1.0 + y * (-1.0 / 6 + y * (1.0 / 120 - y * (1.0 / 5040))))
    cos = 1.0 + y * (-0.5 + y * (1.0 / 24 + y * (-1.0 / 720 + y * (1.0 / 40320))))
    odd = (quarter & 1) == 1
    c = jnp.where(odd, sin, cos)
    s = jnp.where(odd, cos, sin)
    c = jnp.where(((quarter + 1) & 2) == 2, -c, c)
    s = jnp.where((quarter & 2) == 2, -s, s)
    return c, s


def column_shift(step, ox):
    return TILE * (1 - step) - ox


def tile_steps(ctl):
    side = ctl[1]
    return 1 - 2 * side, 2 * side - 1


def lanes():
    return [slice(lane * 128, lane * 128 + 128) for lane in range(TILE // 128)]


def stage(sky, stacked, flipped):
    def kernel(*refs):
        sems = refs[6]
        copies = [pltpu.make_async_copy(refs[i], refs[3 + i], sems.at[i]) for i in range(3)]
        for copy in copies:
            copy.start()
        for copy in copies:
            copy.wait()

    arrays = (sky, stacked, flipped)
    return pl.pallas_call(
        kernel,
        out_shape=[pltpu.VMEM(x.shape, bf16) for x in arrays],
        in_specs=[pl.BlockSpec(memory_space=pltpu.HBM)] * 3,
        out_specs=[pl.BlockSpec(memory_space=pltpu.VMEM)] * 3,
        scratch_shapes=[pltpu.SemaphoreType.DMA((3,))],
        cost_estimate=pl.CostEstimate(flops=0, transcendentals=0, bytes_accessed=18 << 20),
        compiler_params=pltpu.CompilerParams(vmem_limit_bytes=VMEM_LIMIT),
        name="stage",
    )(*[pltpu.with_memory_space_constraint(x, pltpu.HBM) for x in arrays])


def forward_body(low, blocks, slots, meta, stacked, flipped, out, folded, lhs):
    size = 2 * UVB
    begin, end = slots

    def pointing(s, carry):
        oy, ox = meta[OFFSET, s], meta[OFFSET + 1, s]
        width = meta[WIDTH, s].astype(f32)

        def transform(count):
            bins = [(meta[BINS + 2 * k, s], meta[BINS + 2 * k + 1, s]) for k in range(count)]
            g = row_factor_in_lanes(oy, width)
            for k, (a, _) in enumerate(bins):
                rows = slice(k * size, (k + 1) * size)
                table = stacked[a].astype(f32)
                lhs[rows, TILE:] = times_rows(table, g[:, TILE:] * alternating()).astype(bf16)
                lhs[rows, :TILE] = times_rows(table, g[:, :TILE]).astype(bf16)
            parts = [[] for _ in bins]
            for step, (own, pair, far) in blocks:
                shift = column_shift(step, ox)
                first = jnp.dot(lhs[: count * size, TILE:], pair[...], preferred_element_type=f32)
                for at in range(0, TILE, ROWS):
                    here = slice(at, at + ROWS)
                    rows = lax.broadcasted_iota(jnp.int32, (ROWS, TILE), 0) + at
                    mine = jnp.where(rows >= oy, 1, 0) != low
                    both = jnp.where(mine, own[here, :].astype(f32), far[here, :].astype(f32))
                    folded[here, :] = both.astype(bf16)
                first += jnp.dot(lhs[: count * size, :TILE], folded[...], preferred_element_type=f32)
                first = times_rows(first, col_factor(shift, width)).astype(bf16)
                for k, (a, b) in enumerate(bins):
                    rows = first[k * size : (k + 1) * size]
                    q = jnp.dot(rows, flipped[b], preferred_element_type=f32)
                    re = q[:UVB, :UVB] - q[UVB:, UVB:]
                    im = q[:UVB, UVB:] + q[UVB:, :UVB]
                    cos, sin = twiddle(a, b, oy, shift)
                    parts[k].append((re * cos - im * sin, im * cos + re * sin))
            for k, values in enumerate(parts):
                out[s - begin, k, :, :UVB] = sum(re for re, _ in values).astype(out.dtype)
                out[s - begin, k, :, UVB:] = sum(im for _, im in values).astype(out.dtype)

        for count in (1, 2):

            @pl.when(meta[USED, s] == count)
            def _(count=count):
                transform(count)

        return carry

    lax.fori_loop(begin, jnp.minimum(meta[COUNT, 0], end), pointing, 0)


def forward(kind, slots, ctl, meta, skies, stacked, flipped):
    n = len(skies)

    def kernel(ctl, meta, *refs):
        tiles, (stacked, flipped, out, folded, lhs) = refs[: 3 * n], refs[3 * n :]
        near, outer = tile_steps(ctl)
        steps = {"own": (0, -near), "outer": (outer,)}[kind]
        blocks = [(step, tiles[3 * i : 3 * i + 3]) for i, step in enumerate(steps)]
        forward_body(ctl[0], blocks, slots, meta, stacked, flipped, out, folded, lhs)

    smem = pl.BlockSpec(memory_space=pltpu.SMEM)
    vmem = pl.BlockSpec(memory_space=pltpu.VMEM)
    shape = (slots[1] - slots[0], 2, UVB, 2 * UVB)
    return pl.pallas_call(
        kernel,
        out_shape=pltpu.VMEM(shape, f32 if kind == "own" else bf16),
        in_specs=[smem] * 2 + [vmem] * (3 * n + 2),
        out_specs=vmem,
        scratch_shapes=[
            pltpu.VMEM((TILE, TILE), bf16),
            pltpu.VMEM((4 * UVB, PATCH), bf16),
        ],
        cost_estimate=cost(2 * n),
        compiler_params=pltpu.CompilerParams(vmem_limit_bytes=VMEM_LIMIT),
        name="forward_" + kind + str(slots[0]),
    )(ctl, meta, *near_by(*[x for tiles in skies for x in tiles]), stacked, flipped)


def scale(begin, meta, mine, outer, weight):
    def kernel(meta, mine, outer, weight, out):
        def pointing(s, carry):
            def uv(k, c):
                w = weight[s, k].astype(f32)
                v = mine[s, k] + outer[s - begin, k].astype(f32)
                out[s - begin, k, :, :UVB] = (v[:, :UVB] * w).astype(bf16)
                out[s - begin, k, :, UVB:] = (v[:, UVB:] * w).astype(bf16)
                return c

            lax.fori_loop(0, meta[USED, s], uv, 0)
            return carry

        lax.fori_loop(begin, jnp.minimum(meta[COUNT, 0], begin + CHUNK), pointing, 0)

    smem = pl.BlockSpec(memory_space=pltpu.SMEM)
    vmem = pl.BlockSpec(memory_space=pltpu.VMEM)
    return pl.pallas_call(
        kernel,
        out_shape=pltpu.VMEM((CHUNK, 2, UVB, 2 * UVB), bf16),
        in_specs=[smem] + [vmem] * 3,
        out_specs=vmem,
        compiler_params=pltpu.CompilerParams(vmem_limit_bytes=VMEM_LIMIT),
        name="scale" + str(begin),
    )(meta, *near_by(mine, outer, weight))


def adjoint_tile(low, step, begin, meta, scaled, stacked, flipped, spread, totals):
    own, pair, far = totals

    def pointing(s, carry):
        oy, ox = meta[OFFSET, s], meta[OFFSET + 1, s]
        width = meta[WIDTH, s].astype(f32)
        shift = column_shift(step, ox)

        def transform(count):
            bins = [(meta[BINS + 2 * k, s], meta[BINS + 2 * k + 1, s]) for k in range(count)]
            h = col_factor(shift, width)
            for k, (a, b) in enumerate(bins):
                cos, sin = twiddle(a, b, oy, shift)
                re = scaled[s - begin, k, :, :UVB].astype(f32)
                im = scaled[s - begin, k, :, UVB:].astype(f32)
                mr = (re * cos + im * sin).astype(bf16)
                mi = (im * cos - re * sin).astype(bf16)
                both = jnp.concatenate(
                    [jnp.concatenate([mr, mi], axis=1), jnp.concatenate([mi, -mr], axis=1)], axis=0
                )
                value = jnp.dot(both, stacked[b], preferred_element_type=f32)
                spread[0, k] = times_rows(value, h).astype(bf16)
                spread[1, k] = times_rows(value, h * alternating()).astype(bf16)

            def image(at, upper):
                here = slice(at, at + BIG)
                back = jnp.dot(flipped[bins[0][0], here, :], spread[upper, 0], preferred_element_type=f32)
                for k in range(1, count):
                    back += jnp.dot(flipped[bins[k][0], here, :], spread[upper, k], preferred_element_type=f32)
                g, rows = row_factor(at + upper * TILE, BIG, oy, width)
                return [back[:, part] * g for part in lanes()], rows

            for at in range(0, TILE, BIG):
                here = slice(at, at + BIG)
                values, _ = image(at, 1)
                for part, v in zip(lanes(), values):
                    pair[here, part] = pair[here, part] + v
                values, rows = image(at, 0)
                mine = jnp.where(rows >= oy, 1, 0) != low
                for part, v in zip(lanes(), values):
                    own[here, part] = own[here, part] + jnp.where(mine, v, 0.0)
                    far[here, part] = far[here, part] + jnp.where(mine, 0.0, v)

        for count in (1, 2):

            @pl.when(meta[USED, s] == count)
            def _(count=count):
                transform(count)

        return carry

    lax.fori_loop(begin, jnp.minimum(meta[COUNT, 0], begin + CHUNK), pointing, 0)


def adjoint(kind, chunks, ctl, meta, scaled, begun, last, stacked, flipped):
    n = len(scaled)
    started = begun is not None

    def kernel(ctl, meta, *refs):
        scaled, refs = refs[:n], refs[n:]
        totals, refs = (refs[:3], refs[3:]) if started else (None, refs)
        stacked, flipped, *outs, spread = refs
        near, outer = tile_steps(ctl)
        step = {"own": 0, "near": near, "outer": outer}[kind]
        if last:
            totals = (outs[0],) + totals[1:]
        else:
            totals = outs
        if not started:

            def clear(i, c):
                at = pl.multiple_of(i * ROWS, ROWS)
                for ref in totals:
                    ref[pl.ds(at, ROWS), :] = jnp.zeros((ROWS, TILE), f32)
                return c

            lax.fori_loop(0, TILE // ROWS, clear, 0)
        for begin, sc in zip(chunks, scaled):
            adjoint_tile(ctl[0], step, begin, meta, sc, stacked, flipped, spread, totals)
        if last:

            def emit(i, c):
                here = pl.ds(pl.multiple_of(i * ROWS, ROWS), ROWS)
                for total, out in zip(totals[1:], outs[1:]):
                    out[here, :] = total[here, :].astype(bf16)
                return c

            lax.fori_loop(0, TILE // ROWS, emit, 0)

    smem = pl.BlockSpec(memory_space=pltpu.SMEM)
    vmem = pl.BlockSpec(memory_space=pltpu.VMEM)
    first = 2 + n
    aliases = {first: 0} if last else {first + i: i for i in range(3)}
    rest = bf16 if last else f32
    return pl.pallas_call(
        kernel,
        out_shape=[pltpu.VMEM((TILE, TILE), kept) for kept in (f32, rest, rest)],
        in_specs=[smem] * 2 + [vmem] * (n + 2 + (3 if started else 0)),
        out_specs=[vmem] * 3,
        scratch_shapes=[pltpu.VMEM((2, 2, 2 * UVB, TILE), bf16)],
        input_output_aliases=aliases if started else {},
        cost_estimate=cost(2 * n),
        compiler_params=pltpu.CompilerParams(vmem_limit_bytes=VMEM_LIMIT),
        name="adjoint_" + kind + str(chunks[0]),
    )(ctl, meta, *near_by(*scaled, *(begun or ())), stacked, flipped)


def mesh_moves(rows, cols):
    def pairs(move):
        made = []
        for r in range(rows):
            for c in range(cols):
                r2, c2 = move(r, c)
                if 0 <= r2 < rows and 0 <= c2 < cols:
                    made.append((r * cols + c, r2 * cols + c2))
        return made

    def outer(c):
        return c + 1 if c % 2 else c - 1

    return {
        "row_pair": pairs(lambda r, c: (r ^ 1, c)),
        "row_out": pairs(lambda r, c: (r + 2 if r % 2 else r - 2, c)),
        "row_back": pairs(lambda r, c: (r - 2 if r % 2 else r + 2, c)),
        "near": pairs(lambda r, c: (r, c ^ 1)),
        "outer": pairs(lambda r, c: (r, outer(c))),
        "row_pair_near": pairs(lambda r, c: (r ^ 1, c ^ 1)),
        "row_pair_outer": pairs(lambda r, c: (r ^ 1, outer(c))),
    }


def solution(mesh):
    moves = mesh_moves(mesh.shape["ty"], mesh.shape["tx"])
    stacked_np, flipped_np = tables()

    def send(x, what):
        return lax.ppermute(x, ("ty", "tx"), moves[what])

    def shards(sky, point_count, point_offset, beam_width, uv_bins, uv_count, uv_weight):
        ctl = jnp.stack([lax.axis_index("ty") % 2, lax.axis_index("tx") % 2]).astype(jnp.int32)
        rows = (
            (OFFSET, point_offset[0, 0].T),
            (WIDTH, beam_width[0].astype(jnp.int32)),
            (BINS, uv_bins[0, 0].transpose(1, 2, 0).reshape(4, SLOTS)),
            (USED, uv_count[0]),
            (COUNT, jnp.broadcast_to(point_count, (1, SLOTS))),
        )
        meta = sum(jnp.pad(x, ((at, COUNT + 1 - at - x.shape[0]), (0, 0))) for at, x in rows)
        pair_sky = send(sky, "row_pair")
        far_sky = send(sky, "row_out")
        meta_outer = send(meta, "row_pair_outer")
        meta_own = send(meta, "row_pair")
        own_sky, stacked, flipped = stage(sky, jnp.asarray(stacked_np), jnp.asarray(flipped_np))
        weight = send(uv_weight[0, 0], "row_pair")
        skies = (own_sky, pair_sky, far_sky)
        chunks = tuple(range(0, SLOTS, CHUNK))
        from_outer = []
        for begin in chunks:
            v_outer = forward("outer", (begin, begin + CHUNK), ctl, meta_outer, [skies], stacked, flipped)
            from_outer.append(send(v_outer, "outer"))
            meta_outer, v_outer = lax.optimization_barrier((meta_outer, v_outer))
        pair_sky, far_sky, meta_own, weight, meta_outer = lax.optimization_barrier(
            (pair_sky, far_sky, meta_own, weight, meta_outer)
        )
        near_skies = [send(x, "near") for x in (sky, pair_sky, far_sky)]
        meta_near = send(meta_own, "near")
        v_own = forward("own", (0, SLOTS), ctl, meta_own, [skies, near_skies], stacked, flipped)
        scaled = []
        for begin, part in zip(chunks, from_outer):
            scaled.append(scale(begin, meta_own, v_own, part, weight))
            meta_own, _ = lax.optimization_barrier((meta_own, scaled[-1]))
        scaled_outer = [send(x, "outer") for x in scaled]
        scaled_near = [send(x, "near") for x in scaled]
        total = adjoint("own", chunks, ctl, meta_own, scaled, None, False, stacked, flipped)
        total = adjoint("outer", chunks[:1], ctl, meta_outer, scaled_outer[:1], total, False, stacked, flipped)
        total = adjoint("near", chunks, ctl, meta_near, scaled_near, total, False, stacked, flipped)
        total = adjoint("outer", chunks[1:], ctl, meta_outer, scaled_outer[1:], total, True, stacked, flipped)
        own, pair, far = total
        return own + send(pair, "row_pair").astype(f32) + send(far, "row_back").astype(f32)

    in_specs = (
        P("ty", "tx"),
        P("ty", "tx"),
        P("ty", "tx", None, None),
        P("ty", "tx", None),
        P("ty", "tx", None, None, None),
        P("ty", "tx", None),
        P("ty", "tx", None, None, None, None),
    )
    return jax.shard_map(shards, mesh=mesh, in_specs=in_specs, out_specs=P("ty", "tx"), check_vma=False)
```

```python
import math

import jax
import jax.numpy as jnp
import ml_dtypes
import numpy as np
from jax import lax
from jax.experimental import pallas as pl
from jax.experimental.pallas import tpu as pltpu
from jax.sharding import PartitionSpec as P

TILE = 512
PATCH = 1024
UVB = 128
BLOCKS = 8
SLOTS = 4
CHUNK = 2
BIG = 256
HALF = 256
ROWS = 64
VMEM_LIMIT = 24 * 1024 * 1024

OFFSET, WIDTH, BINS, USED, COUNT = 0, 2, 3, 7, 8

f32 = jnp.float32
bf16 = jnp.bfloat16


def tables():
    phase = np.outer(np.arange(PATCH), np.arange(PATCH)) % PATCH
    angle = phase * (2.0 * math.pi / PATCH)
    factor = 1.0 / math.sqrt(PATCH)
    cos = (np.cos(angle) * factor).reshape(BLOCKS, UVB, PATCH)
    sin = (np.sin(angle) * factor).reshape(BLOCKS, UVB, PATCH)
    stacked = np.concatenate([cos, sin], axis=1)
    stacked = stacked[:, :, :TILE]
    flipped = stacked.transpose(0, 2, 1)
    return stacked.astype(ml_dtypes.bfloat16), np.ascontiguousarray(flipped).astype(ml_dtypes.bfloat16)


def near_by(*arrays):
    return [pltpu.with_memory_space_constraint(x, pltpu.VMEM) for x in arrays]


def cost(pointings):
    once = 2 * 2 * UVB * TILE * (PATCH + 2 * UVB)
    return pl.CostEstimate(flops=int(1.5 * pointings * once), transcendentals=0, bytes_accessed=1 << 20)


def falloff(square, width):
    return jnp.exp(square * (-0.5 / (width * width)))


def row_factor(start, rows, oy, width):
    s = lax.broadcasted_iota(jnp.int32, (rows, 128), 0) + start
    m = ((s - oy) & (PATCH - 1)).astype(f32) - (PATCH // 2)
    return falloff(m * m, width), s


def row_factor_in_lanes(oy, width):
    s = lax.broadcasted_iota(jnp.int32, (8, PATCH), 1)
    m = ((s - oy) & (PATCH - 1)).astype(f32) - (PATCH // 2)
    return falloff(m * m, width)


def alternating():
    i = lax.broadcasted_iota(jnp.int32, (8, TILE), 0)
    return jnp.where((i & 1) == 1, -1.0, 1.0).astype(f32)


def times_rows(x, factor):
    return (x.reshape(x.shape[0] // 8, 8, x.shape[1]) * factor[None]).reshape(x.shape)


def half_in_window(step, ox):
    half = ((step == -1) & (ox <= HALF)) | ((step == 1) & (ox >= HALF))
    return half, pl.multiple_of(jnp.where(step == 1, HALF, 0), HALF)


def variants(used, half):
    def run(body):
        for count in (1, 2):
            for narrow in (False, True):

                @pl.when((used == count) & (half == narrow))
                def _(count=count, narrow=narrow):
                    body(count, narrow)

    return run


def col_factor(shift, width, columns):
    n = lax.broadcasted_iota(jnp.int32, (8, columns), 1) + shift
    inside = (n >= 0) & (n < PATCH)
    d = n.astype(f32) - (PATCH // 2)
    return jnp.where(inside, falloff(d * d, width), 0.0)


def twiddle(a, b, oy, shift):
    i = lax.broadcasted_iota(jnp.int32, (UVB, UVB), 0) + a * UVB
    j = lax.broadcasted_iota(jnp.int32, (UVB, UVB), 1) + b * UVB
    p = j * shift - i * oy
    quarter = (p + PATCH // 8) >> 8
    x = (p - (quarter << 8)).astype(f32) * (2.0 * math.pi / PATCH)
    y = x * x
    sin = x * (1.0 + y * (-1.0 / 6 + y * (1.0 / 120 - y * (1.0 / 5040))))
    cos = 1.0 + y * (-0.5 + y * (1.0 / 24 + y * (-1.0 / 720 + y * (1.0 / 40320))))
    odd = (quarter & 1) == 1
    c = jnp.where(odd, sin, cos)
    s = jnp.where(odd, cos, sin)
    c = jnp.where(((quarter + 1) & 2) == 2, -c, c)
    s = jnp.where((quarter & 2) == 2, -s, s)
    return c, s


def column_shift(step, ox):
    return TILE * (1 - step) - ox


def tile_steps(ctl):
    side = ctl[1]
    return 1 - 2 * side, 2 * side - 1


def stage(sky, stacked, flipped):
    def kernel(*refs):
        sems = refs[6]
        copies = [pltpu.make_async_copy(refs[i], refs[3 + i], sems.at[i]) for i in range(3)]
        for copy in copies:
            copy.start()
        for copy in copies:
            copy.wait()

    arrays = (sky, stacked, flipped)
    return pl.pallas_call(
        kernel,
        out_shape=[pltpu.VMEM(x.shape, bf16) for x in arrays],
        in_specs=[pl.BlockSpec(memory_space=pltpu.HBM)] * 3,
        out_specs=[pl.BlockSpec(memory_space=pltpu.VMEM)] * 3,
        scratch_shapes=[pltpu.SemaphoreType.DMA((3,))],
        cost_estimate=pl.CostEstimate(flops=0, transcendentals=0, bytes_accessed=18 << 20),
        compiler_params=pltpu.CompilerParams(vmem_limit_bytes=VMEM_LIMIT),
        name="stage",
    )(*[pltpu.with_memory_space_constraint(x, pltpu.HBM) for x in arrays])


def forward_body(low, blocks, slots, meta, stacked, flipped, out, folded, lhs):
    size = 2 * UVB
    begin, end = slots

    def pointing(s, carry):
        oy, ox = meta[OFFSET, s], meta[OFFSET + 1, s]
        width = meta[WIDTH, s].astype(f32)

        half, start = half_in_window(blocks[-1][0], ox)

        @variants(meta[USED, s], half)
        def transform(count, narrow):
            bins = [(meta[BINS + 2 * k, s], meta[BINS + 2 * k + 1, s]) for k in range(count)]
            g = row_factor_in_lanes(oy, width)
            for k, (a, _) in enumerate(bins):
                rows = slice(k * size, (k + 1) * size)
                table = stacked[a].astype(f32)
                lhs[rows, TILE:] = times_rows(table, g[:, TILE:] * alternating()).astype(bf16)
                lhs[rows, :TILE] = times_rows(table, g[:, :TILE]).astype(bf16)
            parts = [[] for _ in bins]
            for i, (step, (own, pair, far)) in enumerate(blocks):
                cut = narrow and i == len(blocks) - 1
                columns = HALF if cut else TILE
                part = pl.ds(start, HALF) if cut else slice(0, TILE)
                shift = column_shift(step, ox)
                first = jnp.dot(lhs[: count * size, TILE:], pair[:, part], preferred_element_type=f32)
                for at in range(0, TILE, ROWS):
                    here = slice(at, at + ROWS)
                    rows = lax.broadcasted_iota(jnp.int32, (ROWS, columns), 0) + at
                    mine = jnp.where(rows >= oy, 1, 0) != low
                    both = jnp.where(mine, own[here, part].astype(f32), far[here, part].astype(f32))
                    folded[here, :columns] = both.astype(bf16)
                first += jnp.dot(lhs[: count * size, :TILE], folded[:, :columns], preferred_element_type=f32)
                h = col_factor(shift + (start if cut else 0), width, columns)
                first = times_rows(first, h).astype(bf16)
                for k, (a, b) in enumerate(bins):
                    rows = first[k * size : (k + 1) * size]
                    q = jnp.dot(rows, flipped[b, part, :], preferred_element_type=f32)
                    re = q[:UVB, :UVB] - q[UVB:, UVB:]
                    im = q[:UVB, UVB:] + q[UVB:, :UVB]
                    cos, sin = twiddle(a, b, oy, shift)
                    parts[k].append((re * cos - im * sin, im * cos + re * sin))
            for k, values in enumerate(parts):
                out[s - begin, k, :, :UVB] = sum(re for re, _ in values).astype(out.dtype)
                out[s - begin, k, :, UVB:] = sum(im for _, im in values).astype(out.dtype)

        return carry

    lax.fori_loop(begin, jnp.minimum(meta[COUNT, 0], end), pointing, 0)


def forward(kind, slots, ctl, meta, skies, stacked, flipped):
    n = len(skies)

    def kernel(ctl, meta, *refs):
        tiles, (stacked, flipped, out, folded, lhs) = refs[: 3 * n], refs[3 * n :]
        near, outer = tile_steps(ctl)
        steps = {"own": (0, -near), "outer": (outer,)}[kind]
        blocks = [(step, tiles[3 * i : 3 * i + 3]) for i, step in enumerate(steps)]
        forward_body(ctl[0], blocks, slots, meta, stacked, flipped, out, folded, lhs)

    smem = pl.BlockSpec(memory_space=pltpu.SMEM)
    vmem = pl.BlockSpec(memory_space=pltpu.VMEM)
    shape = (slots[1] - slots[0], 2, UVB, 2 * UVB)
    return pl.pallas_call(
        kernel,
        out_shape=pltpu.VMEM(shape, f32 if kind == "own" else bf16),
        in_specs=[smem] * 2 + [vmem] * (3 * n + 2),
        out_specs=vmem,
        scratch_shapes=[
            pltpu.VMEM((TILE, TILE), bf16),
            pltpu.VMEM((4 * UVB, PATCH), bf16),
        ],
        cost_estimate=cost(2 * n),
        compiler_params=pltpu.CompilerParams(vmem_limit_bytes=VMEM_LIMIT),
        name="forward_" + kind + str(slots[0]),
    )(ctl, meta, *near_by(*[x for tiles in skies for x in tiles]), stacked, flipped)


def scale(begin, meta, mine, outer, weight):
    def kernel(meta, mine, outer, weight, out):
        def pointing(s, carry):
            def uv(k, c):
                w = weight[s, k].astype(f32)
                v = mine[s, k] + outer[s - begin, k].astype(f32)
                out[s - begin, k, :, :UVB] = (v[:, :UVB] * w).astype(bf16)
                out[s - begin, k, :, UVB:] = (v[:, UVB:] * w).astype(bf16)
                return c

            lax.fori_loop(0, meta[USED, s], uv, 0)
            return carry

        lax.fori_loop(begin, jnp.minimum(meta[COUNT, 0], begin + CHUNK), pointing, 0)

    smem = pl.BlockSpec(memory_space=pltpu.SMEM)
    vmem = pl.BlockSpec(memory_space=pltpu.VMEM)
    return pl.pallas_call(
        kernel,
        out_shape=pltpu.VMEM((CHUNK, 2, UVB, 2 * UVB), bf16),
        in_specs=[smem] + [vmem] * 3,
        out_specs=vmem,
        compiler_params=pltpu.CompilerParams(vmem_limit_bytes=VMEM_LIMIT),
        name="scale" + str(begin),
    )(meta, *near_by(mine, outer, weight))


def adjoint_tile(low, step, begin, meta, scaled, stacked, flipped, spread, totals):
    own, pair, far = totals

    def pointing(s, carry):
        oy, ox = meta[OFFSET, s], meta[OFFSET + 1, s]
        width = meta[WIDTH, s].astype(f32)
        shift = column_shift(step, ox)

        half, start = half_in_window(step, ox)

        @variants(meta[USED, s], half)
        def transform(count, narrow):
            bins = [(meta[BINS + 2 * k, s], meta[BINS + 2 * k + 1, s]) for k in range(count)]
            columns = HALF if narrow else TILE
            left = start if narrow else 0
            h = col_factor(shift + left, width, columns)
            for k, (a, b) in enumerate(bins):
                cos, sin = twiddle(a, b, oy, shift)
                re = scaled[s - begin, k, :, :UVB].astype(f32)
                im = scaled[s - begin, k, :, UVB:].astype(f32)
                mr = (re * cos + im * sin).astype(bf16)
                mi = (im * cos - re * sin).astype(bf16)
                both = jnp.concatenate(
                    [jnp.concatenate([mr, mi], axis=1), jnp.concatenate([mi, -mr], axis=1)], axis=0
                )
                value = jnp.dot(both, stacked[b, :, pl.ds(left, columns)], preferred_element_type=f32)
                spread[0, k, :, :columns] = times_rows(value, h).astype(bf16)
                spread[1, k, :, :columns] = times_rows(value, h * alternating()[:, :columns]).astype(bf16)

            def image(at, upper):
                here = slice(at, at + BIG)
                back = None
                for k in range(count):
                    part = jnp.dot(
                        flipped[bins[k][0], here, :], spread[upper, k, :, :columns], preferred_element_type=f32
                    )
                    back = part if back is None else back + part
                g, rows = row_factor(at + upper * TILE, BIG, oy, width)
                values = [back[:, lane : lane + 128] * g for lane in range(0, columns, 128)]
                return values, rows

            places = [pl.ds(pl.multiple_of(left + lane, 128), 128) for lane in range(0, columns, 128)]
            for at in range(0, TILE, BIG):
                here = slice(at, at + BIG)
                values, _ = image(at, 1)
                for part, v in zip(places, values):
                    pair[here, part] = pair[here, part] + v
                values, rows = image(at, 0)
                mine = jnp.where(rows >= oy, 1, 0) != low
                for part, v in zip(places, values):
                    own[here, part] = own[here, part] + jnp.where(mine, v, 0.0)
                    far[here, part] = far[here, part] + jnp.where(mine, 0.0, v)

        return carry

    lax.fori_loop(begin, jnp.minimum(meta[COUNT, 0], begin + CHUNK), pointing, 0)


def adjoint(kind, chunks, ctl, meta, scaled, begun, last, stacked, flipped):
    n = len(scaled)
    started = begun is not None

    def kernel(ctl, meta, *refs):
        scaled, refs = refs[:n], refs[n:]
        totals, refs = (refs[:3], refs[3:]) if started else (None, refs)
        stacked, flipped, *outs, spread = refs
        near, outer = tile_steps(ctl)
        step = {"own": 0, "near": near, "outer": outer}[kind]
        if last:
            totals = (outs[0],) + totals[1:]
        else:
            totals = outs
        if not started:

            def clear(i, c):
                at = pl.multiple_of(i * ROWS, ROWS)
                for ref in totals:
                    ref[pl.ds(at, ROWS), :] = jnp.zeros((ROWS, TILE), f32)
                return c

            lax.fori_loop(0, TILE // ROWS, clear, 0)
        for begin, sc in zip(chunks, scaled):
            adjoint_tile(ctl[0], step, begin, meta, sc, stacked, flipped, spread, totals)
        if last:

            def emit(i, c):
                here = pl.ds(pl.multiple_of(i * ROWS, ROWS), ROWS)
                for total, out in zip(totals[1:], outs[1:]):
                    out[here, :] = total[here, :].astype(bf16)
                return c

            lax.fori_loop(0, TILE // ROWS, emit, 0)

    smem = pl.BlockSpec(memory_space=pltpu.SMEM)
    vmem = pl.BlockSpec(memory_space=pltpu.VMEM)
    first = 2 + n
    aliases = {first: 0} if last else {first + i: i for i in range(3)}
    rest = bf16 if last else f32
    return pl.pallas_call(
        kernel,
        out_shape=[pltpu.VMEM((TILE, TILE), kept) for kept in (f32, rest, rest)],
        in_specs=[smem] * 2 + [vmem] * (n + 2 + (3 if started else 0)),
        out_specs=[vmem] * 3,
        scratch_shapes=[pltpu.VMEM((2, 2, 2 * UVB, TILE), bf16)],
        input_output_aliases=aliases if started else {},
        cost_estimate=cost(2 * n),
        compiler_params=pltpu.CompilerParams(vmem_limit_bytes=VMEM_LIMIT),
        name="adjoint_" + kind + str(chunks[0]),
    )(ctl, meta, *near_by(*scaled, *(begun or ())), stacked, flipped)


def mesh_moves(rows, cols):
    def pairs(move):
        made = []
        for r in range(rows):
            for c in range(cols):
                r2, c2 = move(r, c)
                if 0 <= r2 < rows and 0 <= c2 < cols:
                    made.append((r * cols + c, r2 * cols + c2))
        return made

    def outer(c):
        return c + 1 if c % 2 else c - 1

    return {
        "row_pair": pairs(lambda r, c: (r ^ 1, c)),
        "row_out": pairs(lambda r, c: (r + 2 if r % 2 else r - 2, c)),
        "row_back": pairs(lambda r, c: (r - 2 if r % 2 else r + 2, c)),
        "near": pairs(lambda r, c: (r, c ^ 1)),
        "outer": pairs(lambda r, c: (r, outer(c))),
        "row_pair_near": pairs(lambda r, c: (r ^ 1, c ^ 1)),
        "row_pair_outer": pairs(lambda r, c: (r ^ 1, outer(c))),
    }


def solution(mesh):
    moves = mesh_moves(mesh.shape["ty"], mesh.shape["tx"])
    stacked_np, flipped_np = tables()

    def send(x, what):
        return lax.ppermute(x, ("ty", "tx"), moves[what])

    def shards(sky, point_count, point_offset, beam_width, uv_bins, uv_count, uv_weight):
        ctl = jnp.stack([lax.axis_index("ty") % 2, lax.axis_index("tx") % 2]).astype(jnp.int32)
        rows = (
            (OFFSET, point_offset[0, 0].T),
            (WIDTH, beam_width[0].astype(jnp.int32)),
            (BINS, uv_bins[0, 0].transpose(1, 2, 0).reshape(4, SLOTS)),
            (USED, uv_count[0]),
            (COUNT, jnp.broadcast_to(point_count, (1, SLOTS))),
        )
        meta = sum(jnp.pad(x, ((at, COUNT + 1 - at - x.shape[0]), (0, 0))) for at, x in rows)
        pair_sky = send(sky, "row_pair")
        far_sky = send(sky, "row_out")
        meta_outer = send(meta, "row_pair_outer")
        meta_own = send(meta, "row_pair")
        own_sky, stacked, flipped = stage(sky, jnp.asarray(stacked_np), jnp.asarray(flipped_np))
        weight = send(uv_weight[0, 0], "row_pair")
        skies = (own_sky, pair_sky, far_sky)
        meta_near = send(meta, "row_pair_near")
        chunks = tuple(range(0, SLOTS, CHUNK))
        from_outer = []
        for begin in chunks:
            v_outer = forward("outer", (begin, begin + CHUNK), ctl, meta_outer, [skies], stacked, flipped)
            from_outer.append(send(v_outer, "outer"))
            meta_outer, v_outer = lax.optimization_barrier((meta_outer, v_outer))
        pair_sky, far_sky, meta_own, meta_near, weight, meta_outer = lax.optimization_barrier(
            (pair_sky, far_sky, meta_own, meta_near, weight, meta_outer)
        )
        near_skies = [send(x, "near") for x in (sky, pair_sky, far_sky)]
        v_own = forward("own", (0, SLOTS), ctl, meta_own, [skies, near_skies], stacked, flipped)
        scaled = []
        for begin, part in zip(chunks, from_outer):
            scaled.append(scale(begin, meta_own, v_own, part, weight))
            meta_own, _ = lax.optimization_barrier((meta_own, scaled[-1]))
        scaled_outer = [send(x, "outer") for x in scaled]
        scaled_near = [send(x, "near") for x in scaled]
        total = adjoint("own", chunks, ctl, meta_own, scaled, None, False, stacked, flipped)
        total = adjoint("outer", chunks[:1], ctl, meta_outer, scaled_outer[:1], total, False, stacked, flipped)
        total = adjoint("near", chunks, ctl, meta_near, scaled_near, total, False, stacked, flipped)
        total = adjoint("outer", chunks[1:], ctl, meta_outer, scaled_outer[1:], total, True, stacked, flipped)
        own, pair, far = total
        return own + send(pair, "row_pair").astype(f32) + send(far, "row_back").astype(f32)

    in_specs = (
        P("ty", "tx"),
        P("ty", "tx"),
        P("ty", "tx", None, None),
        P("ty", "tx", None),
        P("ty", "tx", None, None, None),
        P("ty", "tx", None),
        P("ty", "tx", None, None, None, None),
    )
    return jax.shard_map(shards, mesh=mesh, in_specs=in_specs, out_specs=P("ty", "tx"), check_vma=False)
```

```python
import math

import jax
import jax.numpy as jnp
import ml_dtypes
import numpy as np
from jax import lax
from jax.experimental import pallas as pl
from jax.experimental.pallas import tpu as pltpu
from jax.sharding import PartitionSpec as P

TILE = 512
PATCH = 1024
UVB = 128
BLOCKS = 8
SLOTS = 4
CHUNK = 2
BIG = 256
HALF = 256
ROWS = 64
VMEM_LIMIT = 24 * 1024 * 1024

OFFSET, WIDTH, BINS, USED, COUNT = 0, 2, 3, 7, 8

f32 = jnp.float32
bf16 = jnp.bfloat16


def tables():
    phase = np.outer(np.arange(PATCH), np.arange(PATCH)) % PATCH
    angle = phase * (2.0 * math.pi / PATCH)
    factor = 1.0 / math.sqrt(PATCH)
    cos = (np.cos(angle) * factor).reshape(BLOCKS, UVB, PATCH)
    sin = (np.sin(angle) * factor).reshape(BLOCKS, UVB, PATCH)
    stacked = np.concatenate([cos, sin], axis=1)
    stacked = stacked[:, :, :TILE]
    flipped = stacked.transpose(0, 2, 1)
    return stacked.astype(ml_dtypes.bfloat16), np.ascontiguousarray(flipped).astype(ml_dtypes.bfloat16)


def near_by(*arrays):
    return [pltpu.with_memory_space_constraint(x, pltpu.VMEM) for x in arrays]


def cost(pointings):
    once = 2 * 2 * UVB * TILE * (PATCH + 2 * UVB)
    return pl.CostEstimate(flops=int(1.5 * pointings * once), transcendentals=0, bytes_accessed=1 << 20)


def falloff(square, width):
    return jnp.exp(square * (-0.5 / (width * width)))


def row_factor(start, rows, oy, width):
    s = lax.broadcasted_iota(jnp.int32, (rows, 128), 0) + start
    m = ((s - oy) & (PATCH - 1)).astype(f32) - (PATCH // 2)
    return falloff(m * m, width), s


def row_factor_in_lanes(oy, width):
    s = lax.broadcasted_iota(jnp.int32, (8, PATCH), 1)
    m = ((s - oy) & (PATCH - 1)).astype(f32) - (PATCH // 2)
    return falloff(m * m, width)


def alternating():
    i = lax.broadcasted_iota(jnp.int32, (8, TILE), 0)
    return jnp.where((i & 1) == 1, -1.0, 1.0).astype(f32)


def times_rows(x, factor):
    return (x.reshape(x.shape[0] // 8, 8, x.shape[1]) * factor[None]).reshape(x.shape)


def half_in_window(step, ox):
    half = ((step == -1) & (ox <= HALF)) | ((step == 1) & (ox >= HALF))
    return half, pl.multiple_of(jnp.where(step == 1, HALF, 0), HALF)


def variants(used, half):
    def run(body):
        for count in (1, 2):
            for narrow in (False, True):

                @pl.when((used == count) & (half == narrow))
                def _(count=count, narrow=narrow):
                    body(count, narrow)

    return run


def col_factor(shift, width, columns):
    n = lax.broadcasted_iota(jnp.int32, (8, columns), 1) + shift
    inside = (n >= 0) & (n < PATCH)
    d = n.astype(f32) - (PATCH // 2)
    return jnp.where(inside, falloff(d * d, width), 0.0)


def twiddle(a, b, oy, shift):
    i = lax.broadcasted_iota(jnp.int32, (UVB, UVB), 0) + a * UVB
    j = lax.broadcasted_iota(jnp.int32, (UVB, UVB), 1) + b * UVB
    p = j * shift - i * oy
    quarter = (p + PATCH // 8) >> 8
    x = (p - (quarter << 8)).astype(f32) * (2.0 * math.pi / PATCH)
    y = x * x
    sin = x * (1.0 + y * (-1.0 / 6 + y * (1.0 / 120 - y * (1.0 / 5040))))
    cos = 1.0 + y * (-0.5 + y * (1.0 / 24 + y * (-1.0 / 720 + y * (1.0 / 40320))))
    odd = (quarter & 1) == 1
    c = jnp.where(odd, sin, cos)
    s = jnp.where(odd, cos, sin)
    c = jnp.where(((quarter + 1) & 2) == 2, -c, c)
    s = jnp.where((quarter & 2) == 2, -s, s)
    return c, s


def column_shift(step, ox):
    return TILE * (1 - step) - ox


def tile_steps(ctl):
    side = ctl[1]
    return 1 - 2 * side, 2 * side - 1


def stage(sky, stacked, flipped):
    def kernel(*refs):
        sems = refs[6]
        copies = [pltpu.make_async_copy(refs[i], refs[3 + i], sems.at[i]) for i in range(3)]
        for copy in copies:
            copy.start()
        for copy in copies:
            copy.wait()

    arrays = (sky, stacked, flipped)
    return pl.pallas_call(
        kernel,
        out_shape=[pltpu.VMEM(x.shape, bf16) for x in arrays],
        in_specs=[pl.BlockSpec(memory_space=pltpu.HBM)] * 3,
        out_specs=[pl.BlockSpec(memory_space=pltpu.VMEM)] * 3,
        scratch_shapes=[pltpu.SemaphoreType.DMA((3,))],
        cost_estimate=pl.CostEstimate(flops=0, transcendentals=0, bytes_accessed=18 << 20),
        compiler_params=pltpu.CompilerParams(vmem_limit_bytes=VMEM_LIMIT),
        name="stage",
    )(*[pltpu.with_memory_space_constraint(x, pltpu.HBM) for x in arrays])


def forward_body(low, blocks, slots, meta, stacked, flipped, out, folded, lhs):
    size = 2 * UVB
    begin, end = slots

    def pointing(s, carry):
        oy, ox = meta[OFFSET, s], meta[OFFSET + 1, s]
        width = meta[WIDTH, s].astype(f32)

        half, start = half_in_window(blocks[-1][0], ox)

        @variants(meta[USED, s], half)
        def transform(count, narrow):
            bins = [(meta[BINS + 2 * k, s], meta[BINS + 2 * k + 1, s]) for k in range(count)]
            g = row_factor_in_lanes(oy, width)
            for k, (a, _) in enumerate(bins):
                rows = slice(k * size, (k + 1) * size)
                table = stacked[a].astype(f32)
                lhs[rows, TILE:] = times_rows(table, g[:, TILE:] * alternating()).astype(bf16)
                lhs[rows, :TILE] = times_rows(table, g[:, :TILE]).astype(bf16)
            parts = [[] for _ in bins]
            for i, (step, (own, pair, far)) in enumerate(blocks):
                cut = narrow and i == len(blocks) - 1
                columns = HALF if cut else TILE
                part = pl.ds(start, HALF) if cut else slice(0, TILE)
                shift = column_shift(step, ox)
                first = jnp.dot(lhs[: count * size, TILE:], pair[:, part], preferred_element_type=f32)
                for at in range(0, TILE, ROWS):
                    here = slice(at, at + ROWS)
                    rows = lax.broadcasted_iota(jnp.int32, (ROWS, columns), 0) + at
                    mine = jnp.where(rows >= oy, 1, 0) != low
                    both = jnp.where(mine, own[here, part].astype(f32), far[here, part].astype(f32))
                    folded[here, :columns] = both.astype(bf16)
                first += jnp.dot(lhs[: count * size, :TILE], folded[:, :columns], preferred_element_type=f32)
                h = col_factor(shift + (start if cut else 0), width, columns)
                first = times_rows(first, h).astype(bf16)
                for k, (a, b) in enumerate(bins):
                    rows = first[k * size : (k + 1) * size]
                    q = jnp.dot(rows, flipped[b, part, :], preferred_element_type=f32)
                    re = q[:UVB, :UVB] - q[UVB:, UVB:]
                    im = q[:UVB, UVB:] + q[UVB:, :UVB]
                    cos, sin = twiddle(a, b, oy, shift)
                    parts[k].append((re * cos - im * sin, im * cos + re * sin))
            for k, values in enumerate(parts):
                out[s - begin, k, :, :UVB] = sum(re for re, _ in values).astype(out.dtype)
                out[s - begin, k, :, UVB:] = sum(im for _, im in values).astype(out.dtype)

        return carry

    lax.fori_loop(begin, jnp.minimum(meta[COUNT, 0], end), pointing, 0)


def forward(kind, slots, ctl, meta, skies, stacked, flipped):
    n = len(skies)

    def kernel(ctl, meta, *refs):
        tiles, (stacked, flipped, out, folded, lhs) = refs[: 3 * n], refs[3 * n :]
        near, outer = tile_steps(ctl)
        steps = {"own": (0, -near), "outer": (outer,)}[kind]
        blocks = [(step, tiles[3 * i : 3 * i + 3]) for i, step in enumerate(steps)]
        forward_body(ctl[0], blocks, slots, meta, stacked, flipped, out, folded, lhs)

    smem = pl.BlockSpec(memory_space=pltpu.SMEM)
    vmem = pl.BlockSpec(memory_space=pltpu.VMEM)
    shape = (slots[1] - slots[0], 2, UVB, 2 * UVB)
    return pl.pallas_call(
        kernel,
        out_shape=pltpu.VMEM(shape, f32 if kind == "own" else bf16),
        in_specs=[smem] * 2 + [vmem] * (3 * n + 2),
        out_specs=vmem,
        scratch_shapes=[
            pltpu.VMEM((TILE, TILE), bf16),
            pltpu.VMEM((4 * UVB, PATCH), bf16),
        ],
        cost_estimate=cost(2 * n),
        compiler_params=pltpu.CompilerParams(vmem_limit_bytes=VMEM_LIMIT),
        name="forward_" + kind + str(slots[0]),
    )(ctl, meta, *near_by(*[x for tiles in skies for x in tiles]), stacked, flipped)


def scale(begin, meta, mine, outer, weight):
    def kernel(meta, mine, outer, weight, out):
        def pointing(s, carry):
            def uv(k, c):
                w = weight[s, k].astype(f32)
                v = mine[s, k] + outer[s, k].astype(f32)
                out[s - begin, k, :, :UVB] = (v[:, :UVB] * w).astype(bf16)
                out[s - begin, k, :, UVB:] = (v[:, UVB:] * w).astype(bf16)
                return c

            lax.fori_loop(0, meta[USED, s], uv, 0)
            return carry

        lax.fori_loop(begin, jnp.minimum(meta[COUNT, 0], begin + CHUNK), pointing, 0)

    smem = pl.BlockSpec(memory_space=pltpu.SMEM)
    vmem = pl.BlockSpec(memory_space=pltpu.VMEM)
    return pl.pallas_call(
        kernel,
        out_shape=pltpu.VMEM((CHUNK, 2, UVB, 2 * UVB), bf16),
        in_specs=[smem] + [vmem] * 3,
        out_specs=vmem,
        compiler_params=pltpu.CompilerParams(vmem_limit_bytes=VMEM_LIMIT),
        name="scale" + str(begin),
    )(meta, *near_by(mine, outer, weight))


def adjoint_tile(low, step, begin, meta, scaled, stacked, flipped, spread, totals):
    own, pair, far = totals

    def pointing(s, carry):
        oy, ox = meta[OFFSET, s], meta[OFFSET + 1, s]
        width = meta[WIDTH, s].astype(f32)
        shift = column_shift(step, ox)

        half, start = half_in_window(step, ox)

        @variants(meta[USED, s], half)
        def transform(count, narrow):
            bins = [(meta[BINS + 2 * k, s], meta[BINS + 2 * k + 1, s]) for k in range(count)]
            columns = HALF if narrow else TILE
            left = start if narrow else 0
            h = col_factor(shift + left, width, columns)
            for k, (a, b) in enumerate(bins):
                cos, sin = twiddle(a, b, oy, shift)
                re = scaled[s - begin, k, :, :UVB].astype(f32)
                im = scaled[s - begin, k, :, UVB:].astype(f32)
                mr = (re * cos + im * sin).astype(bf16)
                mi = (im * cos - re * sin).astype(bf16)
                both = jnp.concatenate(
                    [jnp.concatenate([mr, mi], axis=1), jnp.concatenate([mi, -mr], axis=1)], axis=0
                )
                value = jnp.dot(both, stacked[b, :, pl.ds(left, columns)], preferred_element_type=f32)
                spread[0, k, :, :columns] = times_rows(value, h).astype(bf16)
                spread[1, k, :, :columns] = times_rows(value, h * alternating()[:, :columns]).astype(bf16)

            def image(at, upper):
                here = slice(at, at + BIG)
                back = None
                for k in range(count):
                    part = jnp.dot(
                        flipped[bins[k][0], here, :], spread[upper, k, :, :columns], preferred_element_type=f32
                    )
                    back = part if back is None else back + part
                g, rows = row_factor(at + upper * TILE, BIG, oy, width)
                values = [back[:, lane : lane + 128] * g for lane in range(0, columns, 128)]
                return values, rows

            places = [pl.ds(pl.multiple_of(left + lane, 128), 128) for lane in range(0, columns, 128)]
            for at in range(0, TILE, BIG):
                here = slice(at, at + BIG)
                values, _ = image(at, 1)
                for part, v in zip(places, values):
                    pair[here, part] = pair[here, part] + v
                values, rows = image(at, 0)
                mine = jnp.where(rows >= oy, 1, 0) != low
                for part, v in zip(places, values):
                    own[here, part] = own[here, part] + jnp.where(mine, v, 0.0)
                    far[here, part] = far[here, part] + jnp.where(mine, 0.0, v)

        return carry

    lax.fori_loop(begin, jnp.minimum(meta[COUNT, 0], begin + CHUNK), pointing, 0)


def adjoint(kind, chunks, ctl, meta, scaled, begun, last, stacked, flipped):
    n = len(scaled)
    started = begun is not None

    def kernel(ctl, meta, *refs):
        scaled, refs = refs[:n], refs[n:]
        totals, refs = (refs[:3], refs[3:]) if started else (None, refs)
        stacked, flipped, *outs, spread = refs
        near, outer = tile_steps(ctl)
        step = {"own": 0, "near": near, "outer": outer}[kind]
        if last:
            totals = (outs[0],) + totals[1:]
        else:
            totals = outs
        if not started:

            def clear(i, c):
                at = pl.multiple_of(i * ROWS, ROWS)
                for ref in totals:
                    ref[pl.ds(at, ROWS), :] = jnp.zeros((ROWS, TILE), f32)
                return c

            lax.fori_loop(0, TILE // ROWS, clear, 0)
        for begin, sc in zip(chunks, scaled):
            adjoint_tile(ctl[0], step, begin, meta, sc, stacked, flipped, spread, totals)
        if last:

            def emit(i, c):
                here = pl.ds(pl.multiple_of(i * ROWS, ROWS), ROWS)
                for total, out in zip(totals[1:], outs[1:]):
                    out[here, :] = total[here, :].astype(bf16)
                return c

            lax.fori_loop(0, TILE // ROWS, emit, 0)

    smem = pl.BlockSpec(memory_space=pltpu.SMEM)
    vmem = pl.BlockSpec(memory_space=pltpu.VMEM)
    first = 2 + n
    aliases = {first: 0} if last else {first + i: i for i in range(3)}
    rest = bf16 if last else f32
    return pl.pallas_call(
        kernel,
        out_shape=[pltpu.VMEM((TILE, TILE), kept) for kept in (f32, rest, rest)],
        in_specs=[smem] * 2 + [vmem] * (n + 2 + (3 if started else 0)),
        out_specs=[vmem] * 3,
        scratch_shapes=[pltpu.VMEM((2, 2, 2 * UVB, TILE), bf16)],
        input_output_aliases=aliases if started else {},
        cost_estimate=cost(2 * n),
        compiler_params=pltpu.CompilerParams(vmem_limit_bytes=VMEM_LIMIT),
        name="adjoint_" + kind + str(chunks[0]),
    )(ctl, meta, *near_by(*scaled, *(begun or ())), stacked, flipped)


def mesh_moves(rows, cols):
    def pairs(move):
        made = []
        for r in range(rows):
            for c in range(cols):
                r2, c2 = move(r, c)
                if 0 <= r2 < rows and 0 <= c2 < cols:
                    made.append((r * cols + c, r2 * cols + c2))
        return made

    def outer(c):
        return c + 1 if c % 2 else c - 1

    return {
        "row_pair": pairs(lambda r, c: (r ^ 1, c)),
        "row_out": pairs(lambda r, c: (r + 2 if r % 2 else r - 2, c)),
        "row_back": pairs(lambda r, c: (r - 2 if r % 2 else r + 2, c)),
        "near": pairs(lambda r, c: (r, c ^ 1)),
        "outer": pairs(lambda r, c: (r, outer(c))),
        "row_pair_near": pairs(lambda r, c: (r ^ 1, c ^ 1)),
        "row_pair_outer": pairs(lambda r, c: (r ^ 1, outer(c))),
    }


def solution(mesh):
    moves = mesh_moves(mesh.shape["ty"], mesh.shape["tx"])
    stacked_np, flipped_np = tables()

    def send(x, what):
        return lax.ppermute(x, ("ty", "tx"), moves[what])

    def shards(sky, point_count, point_offset, beam_width, uv_bins, uv_count, uv_weight):
        ctl = jnp.stack([lax.axis_index("ty") % 2, lax.axis_index("tx") % 2]).astype(jnp.int32)
        rows = (
            (OFFSET, point_offset[0, 0].T),
            (WIDTH, beam_width[0].astype(jnp.int32)),
            (BINS, uv_bins[0, 0].transpose(1, 2, 0).reshape(4, SLOTS)),
            (USED, uv_count[0]),
            (COUNT, jnp.broadcast_to(point_count, (1, SLOTS))),
        )
        meta = sum(jnp.pad(x, ((at, COUNT + 1 - at - x.shape[0]), (0, 0))) for at, x in rows)
        pair_sky = send(sky, "row_pair")
        far_sky = send(sky, "row_out")
        meta_outer = send(meta, "row_pair_outer")
        meta_own = send(meta, "row_pair")
        own_sky, stacked, flipped = stage(sky, jnp.asarray(stacked_np), jnp.asarray(flipped_np))
        weight = send(uv_weight[0, 0], "row_pair")
        skies = (own_sky, pair_sky, far_sky)
        meta_near = send(meta, "row_pair_near")
        chunks = tuple(range(0, SLOTS, CHUNK))
        v_outer = forward("outer", (0, SLOTS), ctl, meta_outer, [skies], stacked, flipped)
        from_outer = send(v_outer, "outer")
        meta_outer, v_outer = lax.optimization_barrier((meta_outer, v_outer))
        pair_sky, far_sky, meta_own, meta_near, weight, meta_outer = lax.optimization_barrier(
            (pair_sky, far_sky, meta_own, meta_near, weight, meta_outer)
        )
        near_skies = [send(x, "near") for x in (sky, pair_sky, far_sky)]
        v_own = forward("own", (0, SLOTS), ctl, meta_own, [skies, near_skies], stacked, flipped)
        scaled = []
        for begin in chunks:
            scaled.append(scale(begin, meta_own, v_own, from_outer, weight))
            meta_own, _ = lax.optimization_barrier((meta_own, scaled[-1]))
        scaled_outer = [send(x, "outer") for x in scaled]
        scaled_near = [send(x, "near") for x in scaled]
        total = adjoint("own", chunks, ctl, meta_own, scaled, None, False, stacked, flipped)
        total = adjoint("outer", chunks[:1], ctl, meta_outer, scaled_outer[:1], total, False, stacked, flipped)
        total = adjoint("near", chunks, ctl, meta_near, scaled_near, total, False, stacked, flipped)
        total = adjoint("outer", chunks[1:], ctl, meta_outer, scaled_outer[1:], total, True, stacked, flipped)
        own, pair, far = total
        return own + send(pair, "row_pair").astype(f32) + send(far, "row_back").astype(f32)

    in_specs = (
        P("ty", "tx"),
        P("ty", "tx"),
        P("ty", "tx", None, None),
        P("ty", "tx", None),
        P("ty", "tx", None, None, None),
        P("ty", "tx", None),
        P("ty", "tx", None, None, None, None),
    )
    return jax.shard_map(shards, mesh=mesh, in_specs=in_specs, out_specs=P("ty", "tx"), check_vma=False)
```
